256 devices in a mesh: band: 16 (over y_hi, z), grid: 16 (over x, y_lo, core).
Axes of the slice: x: 4, y: 4 (y_hi: 2, y_lo: 2; y = y_hi * 2 + y_lo), z: 8, core: 2. Of those that a mesh axis runs over, the one named last changes fastest.
Arguments:
- orbitals: float32 [2, 32, 96, 9216], P(None, 'band', 'grid'), may hold values from -7 to 7
- local_potential: float32 [96, 9216], P('grid'), may hold values from 0.5 to 2
- plan: int32 [2], replicated, may hold values from 0 to 15, as said below
- occupancy: int32 [16], replicated, may hold values from 1 to 2, as said below
Outputs:
- new_orbitals: float32 [2, 32, 96, 9216], P(None, 'band', 'grid')
- energies: float32 [32], P('band')
The draws below stay inside these ranges and needn't reach their ends.
Inputs may be any that keep to these rules, and one draw needn't show every extreme that they name: `plan`: distinct band groups, the last group among them. `occupancy`: some group has all 2 orbitals occupied and some group only one.
All inputs are finite; a program needn't handle non-finite values.
Results may differ from the reference program's by a relative error of at most 0.00016.
Values sent between devices are 32-bit elements; how exact they have to be, the bound alone decides.
No kernel may reach another device: no remote copies, remote signals or barrier semaphores. Data moves between devices by JAX's collectives and lax.ppermute only.
A program may use at most 64 MiB of HBM per device.

```python
import math
import jax
import jax.numpy as jnp
from jax import lax

G = 96
OB_DEV = 2
ROUNDS = 2
GROUPS = 16
NORB = 32


def draw_orbitals(key, part):
    base = jax.random.fold_in(key, 37)
    first, second_slope, third = jax.random.split(base, 3)
    along_x = jax.random.randint(first, (NORB,), 0, G).astype(jnp.int32)
    across = jax.random.randint(second_slope, (NORB, 2), 0, max(G // 4, 2)).astype(jnp.int32)
    index = jnp.arange(G, dtype=jnp.int32)
    phase_x = along_x[:, None] * index[None, :] % G
    phase_yz = (across[:, 0][:, None, None] * index[None, :, None] + across[:, 1][:, None, None] * index[None, None, :]) % G
    phase_yz = phase_yz.reshape(NORB, G * G)
    total = (phase_x[:, :, None] + phase_yz[:, None, :]) % G
    rotation_argument = total.astype(jnp.float32) * jnp.float32(2.0 * math.pi / G)
    oscillating_drive = jnp.stack([jnp.cos(rotation_argument), jnp.sin(rotation_argument)])
    approximate_guess = jax.random.normal(third, (2, NORB, G, G * G), jnp.float32)
    drive_strength = 3.0
    return jnp.clip(drive_strength * oscillating_drive + approximate_guess, -7.0, 7.0).astype(jnp.float32)


def draw_plan(key, part):
    order = jax.random.permutation(jax.random.fold_in(key, 11), GROUPS).astype(jnp.int32)
    chosen = order[:ROUNDS]
    present = jnp.any(chosen == GROUPS - 1)
    external_driven = chosen.at[ROUNDS - 1].set(GROUPS - 1)
    return jnp.where(present, chosen, external_driven).astype(jnp.int32)


def draw_occupancy(key, part):
    first, second_slope, third = jax.random.split(jax.random.fold_in(key, 23), 3)
    counts = jax.random.randint(first, (GROUPS,), 1, OB_DEV + 1).astype(jnp.int32)
    full_group = jax.random.randint(second_slope, (), 0, GROUPS)
    low_group = (full_group + 1 + jax.random.randint(third, (), 0, GROUPS - 1)) % GROUPS
    counts = counts.at[full_group].set(OB_DEV)
    counts = counts.at[low_group].set(1)
    return counts.astype(jnp.int32)


def levels(stream_key, shape, cuts, least, largest):
    def one(position, blocks):
        heights = jax.random.uniform(jax.random.fold_in(jax.random.fold_in(stream_key, 6), position), (blocks,), jnp.float32, least / len(cuts), largest / len(cuts))
        return jnp.repeat(jnp.exp(heights), shape[position] // blocks).reshape((-1,) + (1,) * (len(shape) - position - 1))

    loudness = one(*cuts[0])
    for cut in cuts[1:]:
        loudness = loudness * one(*cut)
    return loudness


def setup_inputs(seed: int = 0) -> dict:
    splits = jax.random.split(jax.random.key(seed), 5)
    orbitals = draw_orbitals(jax.random.fold_in(splits[4], 71), 0)
    local_potential = jnp.clip(0.5 + 1.5 * jax.random.uniform(splits[1], (G, G * G), jnp.float32) ** levels(splits[1], (G, G * G), ((0, 16),), -0.2, 0.2), 0.5, 2.0)
    plan = draw_plan(jax.random.fold_in(splits[4], 71), 0)
    occupancy = draw_occupancy(jax.random.fold_in(splits[4], 71), 0)
    return {"orbitals": orbitals, "local_potential": local_potential, "plan": plan, "occupancy": occupancy}


TIME_STEP = 0.4
MIXING = 0.25
OMEGA = 0.106
BOX = 65.1


def screened_kernel(freq_x, freq_y, freq_z):
    def fold(index):
        return jnp.where(index <= G // 2, index, index - G).astype(jnp.float32)
    step = 2.0 * math.pi / BOX
    reduce_first_axis = fold(freq_x)[:, None, None]
    fold_y = fold(freq_y)[None, :, None]
    folded_along_z = fold(freq_z)[None, None, :]
    wave = (step * step) * (reduce_first_axis * reduce_first_axis + fold_y * fold_y + folded_along_z * folded_along_z)
    safe = jnp.where(wave > 0, wave, jnp.float32(1.0))
    screen = -jnp.expm1(-wave / (4.0 * OMEGA * OMEGA)) / safe
    return jnp.where(wave > 0, screen, jnp.float32(1.0 / (4.0 * OMEGA * OMEGA)))


def reference(orbitals, local_potential, plan, occupancy):
    psi = orbitals.reshape(2, NORB, G, G, G)
    field = local_potential.reshape(G, G, G)
    k_first = jnp.stack([field * psi[1], -field * psi[0]])
    section = psi + TIME_STEP * k_first
    axis_index = jnp.arange(G, dtype=jnp.int32)
    kernel = screened_kernel(axis_index, axis_index, axis_index)
    exchange = jnp.zeros_like(section)
    for turn in range(ROUNDS):
        source = plan[turn]
        phi = lax.dynamic_slice_in_dim(section, (source * OB_DEV).astype(jnp.int32), OB_DEV, 1)
        count = occupancy[source]
        weight = jnp.where(jnp.arange(OB_DEV, dtype=jnp.int32) < count, 2.0, 0.0).astype(section.dtype)

        def single(orbital):
            dens_re = phi[0] * orbital[0] + phi[1] * orbital[1]
            dens_im = phi[0] * orbital[1] - phi[1] * orbital[0]
            spectrum = jnp.fft.fftn(dens_re + 1j * dens_im, axes=(1, 2, 3))
            pair = jnp.fft.ifftn(kernel * spectrum, axes=(1, 2, 3))
            pot_re = jnp.real(pair).astype(section.dtype)
            imaginary_potential_part = jnp.imag(pair).astype(section.dtype)
            wide = weight[:, None, None, None]
            term_re = jnp.sum(wide * (phi[0] * pot_re - phi[1] * imaginary_potential_part), axis=0)
            term_im = jnp.sum(wide * (phi[0] * imaginary_potential_part + phi[1] * pot_re), axis=0)
            return -MIXING * jnp.stack([term_re, term_im])

        terms = lax.map(single, jnp.moveaxis(section, 1, 0))
        exchange = exchange + jnp.moveaxis(terms, 0, 1)
    hamil = field * section + exchange
    k_second = jnp.stack([hamil[1], -hamil[0]])
    delta = 0.5 * TIME_STEP * (k_first + k_second)
    along = jnp.sum(psi * delta, axis=(0, 2, 3, 4))
    squared_modulus = jnp.sum(delta * delta, axis=(0, 2, 3, 4))
    energy = jnp.sum(section * hamil, axis=(0, 2, 3, 4))
    factor = -2.0 * along / (squared_modulus + 1e-6)
    fresh = psi + factor[None, :, None, None, None] * delta
    orbital_index = jnp.arange(NORB, dtype=jnp.int32)
    filled = jnp.repeat(occupancy, OB_DEV)
    filling = jnp.where(orbital_index % OB_DEV < filled, 2.0, 0.0).astype(section.dtype)
    return fresh.reshape(2, NORB, G, G * G), filling * energy / (G * G * G)
```

```python
import functools
import math

import jax
import jax.numpy as jnp
import numpy as np
from jax import lax
from jax.experimental import pallas as pl
from jax.experimental.pallas import tpu as pltpu
from jax.sharding import PartitionSpec as P

G = 96
XP = 6
OB = 2
GROUPS = 16
GRID = 16
LANES = G * G
TIME_STEP = 0.4
MIXING = 0.25
OMEGA = 0.106
BOX = 65.1
BF = jnp.bfloat16
F32 = jnp.float32


def tables():
    index = np.arange(G)
    angle = (index[:, None] * index[None, :] % G) * (2.0 * math.pi / G)
    cas = np.cos(angle) + np.sin(angle)
    perm = np.array([6 * (i % 16) + i // 16 for i in range(G)])

    def halves(m):
        hi = np.asarray(m, np.float32).astype(jnp.bfloat16)
        lo = (m - hi.astype(np.float64)).astype(np.float32).astype(jnp.bfloat16)
        return hi, lo

    def extend(m):
        hi, lo = halves(m)
        return np.block([[hi, hi], [lo, np.zeros_like(lo)]])

    pad = np.zeros((4 * 128, 4 * G))
    for f in range(4):
        pad[128 * f : 128 * f + G, G * f : G * f + G] = cas
    return extend(cas[perm]), extend(cas[:, perm]), halves(pad), halves(pad.T)


def split(v):
    hi = v.astype(BF)
    return hi, (v - hi.astype(F32)).astype(BF)


def dot(a, b):
    return jnp.dot(a, b, preferred_element_type=F32)


def left(mat, v):
    hi, lo = split(v)
    p = dot(mat, jnp.concatenate([hi, lo], axis=0))
    return p[:G] + p[G:]


def rows_per_dest(count):
    return -(-3 * 36 * count // 8) * 8


def section_kernel(psi, pot, sec, pay):
    @pl.loop(0, 8)
    def _(q):
        for k in range(9):
            lanes = pl.ds(pl.multiple_of(q * 1152 + k * 128, 128), 128)
            v = TIME_STEP * pot[:, lanes]
            for n in range(OB):
                re, im = psi[0, n, :, lanes], psi[1, n, :, lanes]
                sr, si = re + v * im, im - v * re
                sec[0, n, :, lanes] = sr
                sec[1, n, :, lanes] = si
                rows = pl.ds(56 * n + 6 * k, 6)
                pay[q, rows, :] = sr
                pay[8 + q, rows, :] = si


def source_tiles(big, rel, s, ck, c):
    return [big[rel, c, s, pl.ds(6 * (3 * ck + t), 6), :] for t in range(3)]


def forward_kernel(count, zpos, big, sec, mat, zh, zl, out, tall, yh, yl, res):
    rt = rows_per_dest(count)
    lane = lax.broadcasted_iota(jnp.int32, (XP, 128), 1)

    @pl.loop(0, count)
    def _(s):
        @pl.loop(0, 8)
        def _(q):
            rel = (q + 8 - zpos[0]) & 7
            for ck in range(3):
                pr = source_tiles(big, rel, s, ck, 0)
                pi = source_tiles(big, rel, s, ck, 1)
                base = q * 1152 + ck * 384
                for n in range(OB):
                    parts = [[], []]
                    for t in range(3):
                        lanes = pl.ds(pl.multiple_of(base + 128 * t, 128), 128)
                        sr, si = sec[0, n, :, lanes], sec[1, n, :, lanes]
                        parts[0].append(pr[t] * sr + pi[t] * si)
                        parts[1].append(pr[t] * si - pi[t] * sr)
                    for ri in range(2):
                        a, b, c = parts[ri]
                        ys = [
                            a,
                            jnp.where(lane < 32, pltpu.roll(a, 32, 1), pltpu.roll(b, 32, 1)),
                            jnp.where(lane < 64, pltpu.roll(b, 64, 1), pltpu.roll(c, 64, 1)),
                            pltpu.roll(c, 96, 1),
                        ]
                        for y4 in range(4):
                            row = (q * 12 + ck * 4 + y4) * 32 + 8 * (2 * n + ri)
                            tall[pl.ds(pl.multiple_of(row, 8), XP), :] = ys[y4]
        for x in range(XP):
            v = jnp.concatenate(
                [tall[pl.ds(8 * f + x, G, stride=32), :] for f in range(4)], axis=1
            )
            hi, lo = split(left(mat[...], v))
            yh[pl.ds(G * x, G), :] = hi
            yl[pl.ds(G * x, G), :] = lo
        res[...] = dot(yh[...], zh[...]) + dot(yl[...], zh[...]) + dot(yh[...], zl[...])
        for x in range(XP):
            for k in range(6):
                for t in range(3):
                    out[pl.ds(36 * count * t + 36 * s + 6 * x + k, 16, stride=rt), :] = res[
                        pl.ds(G * x + 16 * k, 16), pl.ds(128 * t, 128)
                    ]


def middle_kernel(count, rec, table, mat1, mat2, out):
    rt = rows_per_dest(count)

    @pl.loop(0, count)
    def _(s):
        for k in range(6):
            starts = [[36 * count * t + 36 * s + 6 * x + k for x in range(XP)] for t in range(3)]
            v = jnp.concatenate(
                [
                    jnp.concatenate(
                        [rec[pl.ds(r, 16, stride=rt), :] for r in starts[t]], axis=0
                    )
                    for t in range(3)
                ],
                axis=1,
            )
            v = left(mat2[...], v) * table[k]
            v = left(mat1[...], v)
            for t in range(3):
                for x in range(XP):
                    out[pl.ds(starts[t][x], 16, stride=rt), :] = v[
                        16 * x : 16 * x + 16, 128 * t : 128 * t + 128
                    ]


def inverse_kernel(
    count, zpos, rec, big, psi, sec, pot, mat, zh, zl, delta, sums, tall, xh, xl, wide, acc
):
    rt = rows_per_dest(count)
    lane = lax.broadcasted_iota(jnp.int32, (XP, 128), 1)
    acc[...] = jnp.zeros_like(acc)

    @pl.loop(0, count)
    def _(s):
        for x in range(XP):
            v = jnp.concatenate(
                [
                    jnp.concatenate(
                        [
                            rec[pl.ds(36 * count * t + 36 * s + 6 * x + k, 16, stride=rt), :]
                            for k in range(6)
                        ],
                        axis=0,
                    )
                    for t in range(3)
                ],
                axis=1,
            )
            hi, lo = split(v)
            xh[pl.ds(G * x, G), :] = hi
            xl[pl.ds(G * x, G), :] = lo
        wide[...] = dot(xh[...], zh[...]) + dot(xl[...], zh[...]) + dot(xh[...], zl[...])
        for x in range(XP):
            v = left(mat[...], wide[pl.ds(G * x, G), :])
            for f in range(4):
                tall[pl.ds(8 * f + x, G, stride=32), :] = v[:, 128 * f : 128 * f + 128]

        @pl.loop(0, 8)
        def _(q):
            rel = (q + 8 - zpos[0]) & 7
            for ck in range(3):
                pr = source_tiles(big, rel, s, ck, 0)
                pi = source_tiles(big, rel, s, ck, 1)
                base = q * 1152 + ck * 384
                for n in range(OB):
                    field = []
                    for ri in range(2):
                        ys = []
                        for y4 in range(4):
                            row = (q * 12 + ck * 4 + y4) * 32 + 8 * (2 * n + ri)
                            ys.append(tall[pl.ds(pl.multiple_of(row, 8), XP), :])
                        r1 = pltpu.roll(ys[1], 96, 1)
                        r2 = pltpu.roll(ys[2], 64, 1)
                        r3 = pltpu.roll(ys[3], 32, 1)
                        field.append(
                            [
                                jnp.where(lane < 96, ys[0], r1),
                                jnp.where(lane < 64, r1, r2),
                                jnp.where(lane < 32, r2, r3),
                            ]
                        )
                    for t in range(3):
                        lanes = pl.ds(pl.multiple_of(base + 128 * t, 128), 128)
                        vr, vi = field[0][t], field[1][t]
                        acc[0, n, :, lanes] += pr[t] * vr - pi[t] * vi
                        acc[1, n, :, lanes] += pr[t] * vi + pi[t] * vr

    def tail(q, carry):
        carry = list(carry)
        for k in range(9):
            lanes = pl.ds(pl.multiple_of(q * 1152 + k * 128, 128), 128)
            v = pot[:, lanes]
            for n in range(OB):
                re, im = psi[0, n, :, lanes], psi[1, n, :, lanes]
                sr, si = sec[0, n, :, lanes], sec[1, n, :, lanes]
                hr = v * sr + acc[0, n, :, lanes]
                hi = v * si + acc[1, n, :, lanes]
                dr = (0.5 * TIME_STEP) * (v * im + hi)
                di = (0.5 * TIME_STEP) * (-v * re - hr)
                delta[0, n, :, lanes] = dr
                delta[1, n, :, lanes] = di
                carry[n] = carry[n] + (re * dr + im * di)
                carry[2 + n] = carry[2 + n] + (dr * dr + di * di)
                carry[4 + n] = carry[4 + n] + (sr * hr + si * hi)
        return tuple(carry)

    zero = jnp.zeros((XP, 128), F32)
    carry = lax.fori_loop(0, 8, tail, (zero,) * 6)
    rows = [jnp.sum(c, axis=0, keepdims=True) for c in carry]
    sums[...] = jnp.concatenate(rows + [jnp.zeros((2, 128), F32)], axis=0)


VM = pl.BlockSpec(memory_space=pltpu.VMEM)
SM = pl.BlockSpec(memory_space=pltpu.SMEM)


def shape(*dims):
    return jax.ShapeDtypeStruct(dims, F32)


def call(kernel, outs, ins, scratch=(), smem=0, flops=0, moved=0):
    return pl.pallas_call(
        kernel,
        out_shape=outs,
        in_specs=[SM] * smem + [VM] * (len(ins) - smem),
        out_specs=[VM] * len(outs),
        scratch_shapes=list(scratch),
        cost_estimate=pl.CostEstimate(flops=flops, bytes_accessed=moved, transcendentals=0),
    )(*ins)


def run_section(psi, pot):
    return call(
        section_kernel, [shape(2, OB, XP, LANES), shape(16, 112, 128)], [psi, pot], moved=3 << 20
    )


def run_forward(count, zpos, big, sec, mat, zh, zl):
    rows = GRID * rows_per_dest(count)
    return call(
        functools.partial(forward_kernel, count),
        [shape(rows, 128)],
        [zpos, big, sec, mat, zh, zl],
        [
            pltpu.VMEM((G * 32, 128), F32),
            pltpu.VMEM((XP * G, 512), BF),
            pltpu.VMEM((XP * G, 512), BF),
            pltpu.VMEM((XP * G, 384), F32),
        ],
        smem=1,
        flops=count << 30,
        moved=count << 21,
    )[0]


def run_middle(count, rec, table, mat1, mat2):
    rows = GRID * rows_per_dest(count)
    return call(
        functools.partial(middle_kernel, count),
        [shape(rows, 128)],
        [rec, table, mat1, mat2],
        flops=count << 30,
        moved=count << 21,
    )[0]


def run_inverse(count, zpos, rec, big, psi, sec, pot, mat, zh, zl):
    return call(
        functools.partial(inverse_kernel, count),
        [shape(2, OB, XP, LANES), shape(8, 128)],
        [zpos, rec, big, psi, sec, pot, mat, zh, zl],
        [
            pltpu.VMEM((G * 32, 128), F32),
            pltpu.VMEM((XP * G, 384), BF),
            pltpu.VMEM((XP * G, 384), BF),
            pltpu.VMEM((XP * G, 512), F32),
            pltpu.VMEM((2, OB, XP, LANES), F32),
        ],
        smem=1,
        flops=count << 30,
        moved=count << 21,
    )


def screened_table(position):
    def fold(index):
        return jnp.where(index <= G // 2, index, index - G).astype(F32)

    step = 2.0 * math.pi / BOX
    fy = fold(6 * position + jnp.arange(6, dtype=jnp.int32))[:, None, None]
    fx = fold(jnp.arange(G, dtype=jnp.int32))[None, :, None]
    fz = fold(jnp.arange(4 * G, dtype=jnp.int32) % G)[None, None, :]
    wave = (step * step) * (fx * fx + fy * fy + fz * fz)
    safe = jnp.where(wave > 0, wave, 1.0)
    screen = -jnp.expm1(-wave / (4.0 * OMEGA * OMEGA)) / safe
    screen = jnp.where(wave > 0, screen, 1.0 / (4.0 * OMEGA * OMEGA))
    return screen * (-2.0 * MIXING / (G * G * G))


RIGHT = [(h * 8 + z, h * 8 + (z + 1) % 8) for h in range(2) for z in range(8)]
LEFT = [(d, s) for s, d in RIGHT]
SWAP = [(i, i ^ 8) for i in range(16)]


def gather_sources(pieces, upper):
    hop = lambda v, pairs: lax.ppermute(v, "band", pairs)
    other = hop(pieces, SWAP)
    both = jnp.where(upper, jnp.stack([other, pieces]), jnp.stack([pieces, other]))
    r1, l1 = hop(both, RIGHT), hop(both, LEFT)
    r2, l2 = hop(r1, RIGHT), hop(l1, LEFT)
    r3, l3 = hop(r2, RIGHT), hop(l2, LEFT)
    far = jnp.stack([hop(r3[0], RIGHT), hop(l3[1], LEFT)])
    return jnp.stack([both, l1, l2, l3, far, r3, r2, r1])


def per_device(orbitals, local_potential, plan, occupancy):
    group = jnp.arange(GROUPS, dtype=jnp.int32)
    lookup = lambda g: jnp.sum(jnp.where(group == g, occupancy, 0))
    band = lax.axis_index("band")
    zpos = (band % 8).astype(jnp.int32).reshape(1)
    mat1, mat2, (zfh, zfl), (zih, zil) = [
        jax.tree.map(jnp.asarray, t) for t in tables()
    ]
    table = screened_table(lax.axis_index("grid"))
    sec, pay = run_section(orbitals, local_potential)
    pool = lax.all_to_all(pay, "band", 0, 0, tiled=True)
    first, second = lookup(plan[0]), lookup(plan[1])
    third = jnp.where(first > 1, plan[0], plan[1])
    slots = [(plan[0], 0), (plan[1], 0), (third, 1), (plan[1], 1)]

    def branch(count):
        def run(orbitals, local_potential, sec, pool, table, slot_groups):
            pieces = jnp.stack(
                [
                    lax.dynamic_slice(pool, (slot_groups[i], 56 * slots[i][1], 0), (1, 56, 128))[0]
                    for i in range(count)
                ]
            )
            big = gather_sources(pieces, band >= 8)
            send = run_forward(count, zpos, big, sec, mat1, zfh, zfl)
            got = lax.all_to_all(send, "grid", 0, 0, tiled=True)
            back = run_middle(count, got, table, mat1, mat2)
            got = lax.all_to_all(back, "grid", 0, 0, tiled=True)
            return tuple(
                run_inverse(
                    count, zpos, got, big, orbitals, sec, local_potential, mat2, zih, zil
                )
            )

        return run

    slot_groups = jnp.stack([g for g, _ in slots])
    delta, sums = lax.switch(
        first + second - 2,
        [branch(2), branch(3), branch(4)],
        orbitals,
        local_potential,
        sec,
        pool,
        table,
        slot_groups,
    )
    spread = jnp.broadcast_to(sums[None], (GRID, 8, 128))
    total = jnp.sum(lax.all_to_all(spread, "grid", 0, 0, tiled=True), axis=(0, 2))
    along, squared, energy = total[0:2], total[2:4], total[4:6]
    factor = -2.0 * along / (squared + 1e-06)
    fresh = orbitals + factor[None, :, None, None] * delta
    own_filled = lookup(band)
    filling = jnp.where(jnp.arange(OB, dtype=jnp.int32) < own_filled, 2.0, 0.0).astype(F32)
    return (fresh, filling * energy / (G * G * G))


def solution(mesh):
    return jax.shard_map(
        per_device,
        mesh=mesh,
        in_specs=(P(None, "band", "grid", None), P("grid", None), P(), P()),
        out_specs=(P(None, "band", "grid", None), P("band")),
        check_vma=False,
    )
```

```python
import functools
import math

import jax
import jax.numpy as jnp
import numpy as np
from jax import lax
from jax.experimental import pallas as pl
from jax.experimental.pallas import tpu as pltpu
from jax.sharding import PartitionSpec as P

G = 96
XP = 6
OB = 2
GROUPS = 16
GRID = 16
LANES = G * G
TIME_STEP = 0.4
MIXING = 0.25
OMEGA = 0.106
BOX = 65.1
BF = jnp.bfloat16
F32 = jnp.float32


def tables():
    index = np.arange(G)
    angle = (index[:, None] * index[None, :] % G) * (2.0 * math.pi / G)
    cas = np.cos(angle) + np.sin(angle)
    perm = np.array([6 * (i % 16) + i // 16 for i in range(G)])

    def halves(m):
        hi = np.asarray(m, np.float32).astype(jnp.bfloat16)
        lo = (m - hi.astype(np.float64)).astype(np.float32).astype(jnp.bfloat16)
        return hi, lo

    def extend(m):
        hi, lo = halves(m)
        return np.block([[hi, hi], [lo, np.zeros_like(lo)]])

    pads = [np.pad(h.astype(np.float32), (0, 128 - G)) for h in halves(cas)]
    return extend(cas[perm]), extend(cas[:, perm]), pads


def split(v):
    hi = v.astype(BF)
    return hi, (v - hi.astype(F32)).astype(BF)


def dot(a, b):
    return jnp.dot(a, b, preferred_element_type=F32)


def left(mat, v):
    hi, lo = split(v)
    p = dot(mat, jnp.concatenate([hi, lo], axis=0))
    return p[:G] + p[G:]


def rows_per_dest(count):
    return -(-3 * 36 * count // 8) * 8


def orbital_rows(c, n, t):
    return pl.ds(c * 864 + 2 * t + n, XP, stride=144)


def prepare_kernel(hi, lo, wf, wi):
    zero = jnp.zeros((128, 128), BF)
    for f in range(4):
        for axis, out in ((1, wf), (0, wi)):
            shift = 96 * f % 128
            h = (pltpu.roll(hi[...], shift, axis) if shift else hi[...]).astype(BF)
            l = (pltpu.roll(lo[...], shift, axis) if shift else lo[...]).astype(BF)
            out[f, 0:128, 0:128] = h
            out[f, 128:256, 0:128] = h
            out[f, 0:128, 128:256] = l
            out[f, 128:256, 128:256] = zero


def section_kernel(psi, pot, sec, pay):
    @pl.loop(0, 8)
    def _(q):
        for k in range(9):
            t = q * 9 + k
            lanes = pl.ds(pl.multiple_of(t * 128, 128), 128)
            v = TIME_STEP * pot[:, lanes]
            for n in range(OB):
                re, im = psi[orbital_rows(0, n, t), :], psi[orbital_rows(1, n, t), :]
                sr, si = re + v * im, im - v * re
                sec[0, n, :, lanes] = sr
                sec[1, n, :, lanes] = si
                rows = pl.ds(56 * n + 6 * k, 6)
                pay[q, rows, :] = sr
                pay[8 + q, rows, :] = si


def source_tiles(big, rel, s, ck, c):
    return [big[rel, c, s, pl.ds(6 * (3 * ck + t), 6), :] for t in range(3)]


def forward_kernel(count, zpos, big, sec, mat, wf, out, tall, yw, held):
    rt = rows_per_dest(count)
    lane = lax.broadcasted_iota(jnp.int32, (XP, 128), 1)
    lane16 = lax.broadcasted_iota(jnp.int32, (16, 128), 1)

    @pl.loop(0, count)
    def _(s):
        @pl.loop(0, 4)
        def _(half):
            for q in (half, half + 4):
                rel = (q + 8 - zpos[0]) & 7
                for ck in range(3):
                    pr = source_tiles(big, rel, s, ck, 0)
                    pi = source_tiles(big, rel, s, ck, 1)
                    base = q * 1152 + ck * 384
                    for n in range(OB):
                        parts = [[], []]
                        for t in range(3):
                            lanes = pl.ds(pl.multiple_of(base + 128 * t, 128), 128)
                            sr, si = sec[0, n, :, lanes], sec[1, n, :, lanes]
                            parts[0].append(pr[t] * sr + pi[t] * si)
                            parts[1].append(pr[t] * si - pi[t] * sr)
                        for ri in range(2):
                            a, b, c = parts[ri]
                            ys = [
                                a,
                                pltpu.roll(jnp.where(lane < 96, b, a), 32, 1),
                                pltpu.roll(jnp.where(lane < 64, c, b), 64, 1),
                                pltpu.roll(c, 96, 1),
                            ]
                            for y4 in range(4):
                                row = (q * 12 + ck * 4 + y4) * 32 + 8 * (2 * n + ri)
                                tall[pl.ds(pl.multiple_of(row, 8), XP), :] = ys[y4]

        for x in range(XP):
            v = jnp.concatenate(
                [tall[pl.ds(8 * f + x, G, stride=32), :] for f in range(4)], axis=1
            )
            hi, lo = split(left(mat[...], v))
            for f in range(4):
                yw[f, pl.ds(G * x, G), 0:128] = hi[:, 128 * f : 128 * f + 128]
                yw[f, pl.ds(G * x, G), 128:256] = lo[:, 128 * f : 128 * f + 128]
        for f in range(4):
            p = dot(yw[f], wf[f])
            p = p[:, 0:128] + p[:, 128:256]
            if f:
                edge = 128 - 32 * f
                for x in range(XP):
                    for k in range(6):
                        r = G * x + 16 * k
                        start = 36 * count * (f - 1) + 36 * s + 6 * x + k
                        out[pl.ds(start, 16, stride=rt), :] = jnp.where(
                            lane16 < edge, held[pl.ds(r, 16), :], p[r : r + 16]
                        )
            if f < 3:
                held[...] = p


def middle_kernel(count, rec, table, mat1, mat2, out):
    rt = rows_per_dest(count)

    @pl.loop(0, count)
    def _(s):
        for kk in range(3):
            starts = [
                [36 * count * t + 36 * s + 6 * x + k for x in range(XP)]
                for k in (2 * kk, 2 * kk + 1)
                for t in range(3)
            ]
            v = jnp.concatenate(
                [
                    jnp.concatenate([rec[pl.ds(r, 16, stride=rt), :] for r in st], axis=0)
                    for st in starts
                ],
                axis=1,
            )
            v = left(mat2[...], v) * jnp.concatenate([table[2 * kk], table[2 * kk + 1]], axis=1)
            v = left(mat1[...], v)
            for i, st in enumerate(starts):
                for x in range(XP):
                    out[pl.ds(st[x], 16, stride=rt), :] = v[
                        16 * x : 16 * x + 16, 128 * i : 128 * i + 128
                    ]


def inverse_kernel(
    count, zpos, rec, big, psi, sec, pot, mat, wi, delta, sums, tall, xw, wide, acc
):
    rt = rows_per_dest(count)
    lane = lax.broadcasted_iota(jnp.int32, (XP, 128), 1)
    laneg = lax.broadcasted_iota(jnp.int32, (G, 128), 1)
    acc[...] = jnp.zeros_like(acc)

    @pl.loop(0, count)
    def _(s):
        for x in range(XP):
            a, b, c = [
                jnp.concatenate(
                    [
                        rec[pl.ds(36 * count * t + 36 * s + 6 * x + k, 16, stride=rt), :]
                        for k in range(6)
                    ],
                    axis=0,
                )
                for t in range(3)
            ]
            fields = [a, jnp.where(laneg < 64, b, a), jnp.where(laneg < 32, c, b), c]
            for f in range(4):
                hi, lo = split(fields[f])
                xw[f, pl.ds(G * x, G), 0:128] = hi
                xw[f, pl.ds(G * x, G), 128:256] = lo
        for f in range(4):
            p = dot(xw[f], wi[f])
            wide[f] = p[:, 0:128] + p[:, 128:256]
        for x in range(XP):
            v = jnp.concatenate([wide[f, pl.ds(G * x, G), :] for f in range(4)], axis=1)
            v = left(mat[...], v)
            for f in range(4):
                tall[pl.ds(8 * f + x, G, stride=32), :] = v[:, 128 * f : 128 * f + 128]

        @pl.loop(0, 4)
        def _(half):
            for q in (half, half + 4):
                rel = (q + 8 - zpos[0]) & 7
                for ck in range(3):
                    pr = source_tiles(big, rel, s, ck, 0)
                    pi = source_tiles(big, rel, s, ck, 1)
                    base = q * 1152 + ck * 384
                    for n in range(OB):
                        field = []
                        for ri in range(2):
                            ys = []
                            for y4 in range(4):
                                row = (q * 12 + ck * 4 + y4) * 32 + 8 * (2 * n + ri)
                                ys.append(tall[pl.ds(pl.multiple_of(row, 8), XP), :])
                            r1 = pltpu.roll(ys[1], 96, 1)
                            r2 = pltpu.roll(ys[2], 64, 1)
                            r3 = pltpu.roll(ys[3], 32, 1)
                            field.append(
                                [
                                    jnp.where(lane < 96, ys[0], r1),
                                    jnp.where(lane < 64, r1, r2),
                                    jnp.where(lane < 32, r2, r3),
                                ]
                            )
                        for t in range(3):
                            lanes = pl.ds(pl.multiple_of(base + 128 * t, 128), 128)
                            vr, vi = field[0][t], field[1][t]
                            acc[0, n, :, lanes] += pr[t] * vr - pi[t] * vi
                            acc[1, n, :, lanes] += pr[t] * vi + pi[t] * vr

    def tail(q, carry):
        carry = list(carry)
        for k in range(9):
            t = q * 9 + k
            lanes = pl.ds(pl.multiple_of(t * 128, 128), 128)
            v = pot[:, lanes]
            for n in range(OB):
                re, im = psi[orbital_rows(0, n, t), :], psi[orbital_rows(1, n, t), :]
                sr, si = sec[0, n, :, lanes], sec[1, n, :, lanes]
                hr = v * sr + acc[0, n, :, lanes]
                hi = v * si + acc[1, n, :, lanes]
                dr = (0.5 * TIME_STEP) * (v * im + hi)
                di = (0.5 * TIME_STEP) * (-v * re - hr)
                delta[orbital_rows(0, n, t), :] = dr
                delta[orbital_rows(1, n, t), :] = di
                carry[n] = carry[n] + (re * dr + im * di)
                carry[2 + n] = carry[2 + n] + (dr * dr + di * di)
                carry[4 + n] = carry[4 + n] + (sr * hr + si * hi)
        return tuple(carry)

    zero = jnp.zeros((XP, 128), F32)
    carry = lax.fori_loop(0, 8, tail, (zero,) * 6)
    rows = [jnp.sum(c, axis=0, keepdims=True) for c in carry]
    sums[...] = jnp.concatenate(rows + [jnp.zeros((2, 128), F32)], axis=0)


VM = pl.BlockSpec(memory_space=pltpu.VMEM)
SM = pl.BlockSpec(memory_space=pltpu.SMEM)


def shape(*dims):
    return jax.ShapeDtypeStruct(dims, F32)


def call(kernel, outs, ins, scratch=(), smem=0, flops=0, moved=0):
    return pl.pallas_call(
        kernel,
        out_shape=outs,
        in_specs=[SM] * smem + [VM] * (len(ins) - smem),
        out_specs=[VM] * len(outs),
        scratch_shapes=list(scratch),
        cost_estimate=pl.CostEstimate(flops=flops, bytes_accessed=moved, transcendentals=0),
    )(*ins)


def run_prepare(hi, lo):
    wide = jax.ShapeDtypeStruct((4, 256, 256), BF)
    return call(prepare_kernel, [wide, wide], [hi, lo], moved=2 << 20)


def run_section(psi, pot):
    return call(
        section_kernel, [shape(2, OB, XP, LANES), shape(16, 112, 128)], [psi, pot], moved=3 << 20
    )


def run_forward(count, zpos, big, sec, mat, wf):
    rows = GRID * rows_per_dest(count)
    return call(
        functools.partial(forward_kernel, count),
        [shape(rows, 128)],
        [zpos, big, sec, mat, wf],
        [
            pltpu.VMEM((G * 32, 128), F32),
            pltpu.VMEM((4, XP * G, 256), BF),
            pltpu.VMEM((XP * G, 128), F32),
        ],
        smem=1,
        flops=count << 30,
        moved=count << 21,
    )[0]


def run_middle(count, rec, table, mat1, mat2):
    rows = GRID * rows_per_dest(count)
    return call(
        functools.partial(middle_kernel, count),
        [shape(rows, 128)],
        [rec, table, mat1, mat2],
        flops=count << 30,
        moved=count << 21,
    )[0]


def run_inverse(count, zpos, rec, big, psi, sec, pot, mat, wi):
    return call(
        functools.partial(inverse_kernel, count),
        [shape(2 * XP * 144, 128), shape(8, 128)],
        [zpos, rec, big, psi, sec, pot, mat, wi],
        [
            pltpu.VMEM((G * 32, 128), F32),
            pltpu.VMEM((4, XP * G, 256), BF),
            pltpu.VMEM((4, XP * G, 128), F32),
            pltpu.VMEM((2, OB, XP, LANES), F32),
        ],
        smem=1,
        flops=count << 30,
        moved=count << 21,
    )


def screened_table(position):
    def fold(index):
        return jnp.where(index <= G // 2, index, index - G).astype(F32)

    step = 2.0 * math.pi / BOX
    fy = fold(6 * position + jnp.arange(6, dtype=jnp.int32))[:, None, None]
    fx = fold(jnp.arange(G, dtype=jnp.int32))[None, :, None]
    fz = fold(jnp.arange(4 * G, dtype=jnp.int32) % G)[None, None, :]
    wave = (step * step) * (fx * fx + fy * fy + fz * fz)
    safe = jnp.where(wave > 0, wave, 1.0)
    screen = -jnp.expm1(-wave / (4.0 * OMEGA * OMEGA)) / safe
    screen = jnp.where(wave > 0, screen, 1.0 / (4.0 * OMEGA * OMEGA))
    return screen * (-2.0 * MIXING / (G * G * G))


RIGHT = [(h * 8 + z, h * 8 + (z + 1) % 8) for h in range(2) for z in range(8)]
LEFT = [(d, s) for s, d in RIGHT]
SWAP = [(i, i ^ 8) for i in range(16)]


def gather_sources(pieces, upper):
    hop = lambda v, pairs: lax.ppermute(v, "band", pairs)
    other = hop(pieces, SWAP)
    both = jnp.where(upper, jnp.stack([other, pieces]), jnp.stack([pieces, other]))
    r1, l1 = hop(both, RIGHT), hop(both, LEFT)
    r2, l2 = hop(r1, RIGHT), hop(l1, LEFT)
    r3, l3 = hop(r2, RIGHT), hop(l2, LEFT)
    far = jnp.stack([hop(r3[0], RIGHT), hop(l3[1], LEFT)])
    return jnp.stack([both, l1, l2, l3, far, r3, r2, r1])


def per_device(orbitals, local_potential, plan, occupancy):
    group = jnp.arange(GROUPS, dtype=jnp.int32)
    lookup = lambda g: jnp.sum(jnp.where(group == g, occupancy, 0))
    band = lax.axis_index("band")
    zpos = (band % 8).astype(jnp.int32).reshape(1)
    mat1, mat2, (hi, lo) = jax.tree.map(jnp.asarray, tables())
    wf, wi = run_prepare(hi, lo)
    tiled = orbitals.reshape(2, OB, XP, 72, 128).transpose(0, 2, 3, 1, 4).reshape(-1, 128)
    table = screened_table(lax.axis_index("grid"))
    sec, pay = run_section(tiled, local_potential)
    pool = lax.all_to_all(pay, "band", 0, 0, tiled=True)
    first, second = lookup(plan[0]), lookup(plan[1])
    third = jnp.where(first > 1, plan[0], plan[1])
    slots = [(plan[0], 0), (plan[1], 0), (third, 1), (plan[1], 1)]

    def branch(count):
        def run(tiled, local_potential, sec, pool, table, wf, wi, slot_groups):
            pieces = jnp.stack(
                [
                    lax.dynamic_slice(pool, (slot_groups[i], 56 * slots[i][1], 0), (1, 56, 128))[0]
                    for i in range(count)
                ]
            )
            big = gather_sources(pieces, band >= 8)
            send = run_forward(count, zpos, big, sec, mat1, wf)
            got = lax.all_to_all(send, "grid", 0, 0, tiled=True)
            back = run_middle(count, got, table, mat1, mat2)
            got = lax.all_to_all(back, "grid", 0, 0, tiled=True)
            return tuple(
                run_inverse(count, zpos, got, big, tiled, sec, local_potential, mat2, wi)
            )

        return run

    slot_groups = jnp.stack([g for g, _ in slots])
    delta, sums = lax.switch(
        first + second - 2,
        [branch(2), branch(3), branch(4)],
        tiled,
        local_potential,
        sec,
        pool,
        table,
        wf,
        wi,
        slot_groups,
    )
    spread = jnp.broadcast_to(sums[None], (GRID, 8, 128))
    total = jnp.sum(lax.all_to_all(spread, "grid", 0, 0, tiled=True), axis=(0, 2))
    along, squared, energy = total[0:2], total[2:4], total[4:6]
    factor = -2.0 * along / (squared + 1e-06)
    odd = lax.broadcasted_iota(jnp.int32, tiled.shape, 0) % OB == 1
    fresh = tiled + jnp.where(odd, factor[1], factor[0]) * delta
    fresh = fresh.reshape(2, XP, 72, OB, 128)
    fresh = fresh.transpose(0, 3, 1, 2, 4).reshape(orbitals.shape)
    own_filled = lookup(band)
    filling = jnp.where(jnp.arange(OB, dtype=jnp.int32) < own_filled, 2.0, 0.0).astype(F32)
    return (fresh, filling * energy / (G * G * G))


def solution(mesh):
    return jax.shard_map(
        per_device,
        mesh=mesh,
        in_specs=(P(None, "band", "grid", None), P("grid", None), P(), P()),
        out_specs=(P(None, "band", "grid", None), P("band")),
        check_vma=False,
    )
```

```python
import functools
import math

import jax
import jax.numpy as jnp
import numpy as np
from jax import lax
from jax.experimental import pallas as pl
from jax.experimental.pallas import tpu as pltpu
from jax.sharding import PartitionSpec as P

G = 96
XP = 6
OB = 2
GROUPS = 16
GRID = 16
LANES = G * G
TIME_STEP = 0.4
MIXING = 0.25
OMEGA = 0.106
BOX = 65.1
BF = jnp.bfloat16
F32 = jnp.float32


def tables():
    index = np.arange(G)
    angle = (index[:, None] * index[None, :] % G) * (2.0 * math.pi / G)
    cas = np.cos(angle) + np.sin(angle)
    perm = np.array([6 * (i % 16) + i // 16 for i in range(G)])

    def halves(m):
        hi = np.asarray(m, np.float32).astype(jnp.bfloat16)
        lo = (m - hi.astype(np.float64)).astype(np.float32).astype(jnp.bfloat16)
        return hi, lo

    def extend(m):
        hi, lo = halves(m)
        return np.block([[hi, hi], [lo, np.zeros_like(lo)]])

    rows = np.array([4 * (i % 24) + i // 24 for i in range(G)])
    pads = [np.pad(h.astype(np.float32), (0, 128 - G)) for h in halves(cas)]
    mats = [cas[perm][:, rows], cas[:, perm], cas[perm], cas[rows][:, perm]]
    return [extend(m) for m in mats], pads


def split(v):
    hi = v.astype(BF)
    return hi, (v - hi.astype(F32)).astype(BF)


def dot(a, b):
    return jnp.dot(a, b, preferred_element_type=F32)


def left(mat, v):
    hi, lo = split(v)
    p = dot(mat, jnp.concatenate([hi, lo], axis=0))
    return p[:G] + p[G:]


def rows_per_dest(count):
    return -(-3 * 36 * count // 8) * 8


def prepare_kernel(hi, lo, wf, wi):
    zero = jnp.zeros((128, 128), BF)
    for f in range(4):
        for axis, out in ((1, wf), (0, wi)):
            shift = 96 * f % 128
            h = (pltpu.roll(hi[...], shift, axis) if shift else hi[...]).astype(BF)
            l = (pltpu.roll(lo[...], shift, axis) if shift else lo[...]).astype(BF)
            out[f, 0:128, 0:128] = h
            out[f, 128:256, 0:128] = h
            out[f, 0:128, 128:256] = l
            out[f, 128:256, 128:256] = zero


def section_kernel(psi, pot, sec, image, potim, pay):
    for t in range(72):
        a, b = t // 3, t % 3
        potim[pl.ds(24 * b + a, XP, stride=72), :] = pot[:, 128 * t : 128 * t + 128]

    @pl.loop(0, XP)
    def _(x):
        for b in range(3):
            rows = pl.ds(pl.multiple_of(72 * x + 24 * b, 8), 24)
            v = TIME_STEP * potim[rows, :]
            for n in range(OB):
                re, im = [
                    psi[pl.ds((c * XP + x) * 144 + 2 * b + n, 24, stride=6), :] for c in range(2)
                ]
                sec[0, n, rows, :] = re + v * im
                sec[1, n, rows, :] = im - v * re
                image[0, n, rows, :] = re
                image[1, n, rows, :] = im

    for c in range(2):
        for n in range(OB):
            for q in range(8):
                pay[8 * c + q, 56 * n : 56 * n + 54, :] = sec[c, n, 54 * q : 54 * q + 54, :]


def assemble(where, big, s, phi):
    for c in range(2):
        for q in range(8):
            rel = (q + 8 - where[0]) & 7
            phi[c, 54 * q : 54 * q + 54, :] = big[rel, c ^ where[1], s, 0:54, :]


def forward_kernel(count, where, big, sec, mat, wf, out, phi, yw, held):
    rt = rows_per_dest(count)
    lane = lax.broadcasted_iota(jnp.int32, (24, 128), 1)
    lane16 = lax.broadcasted_iota(jnp.int32, (16, 128), 1)

    @pl.loop(0, count)
    def _(s):
        assemble(where, big, s, phi)
        for x in range(XP):
            rows = [pl.ds(72 * x + 24 * b, 24) for b in range(3)]
            pr = [phi[0, r, :] for r in rows]
            pi = [phi[1, r, :] for r in rows]
            columns = []
            for n in range(OB):
                sr = [sec[0, n, r, :] for r in rows]
                si = [sec[1, n, r, :] for r in rows]
                for part in (
                    [pr[b] * sr[b] + pi[b] * si[b] for b in range(3)],
                    [pr[b] * si[b] - pi[b] * sr[b] for b in range(3)],
                ):
                    a, b, c = part
                    columns.append(
                        jnp.concatenate(
                            [
                                a,
                                pltpu.roll(jnp.where(lane < 96, b, a), 32, 1),
                                pltpu.roll(jnp.where(lane < 64, c, b), 64, 1),
                                pltpu.roll(c, 96, 1),
                            ],
                            axis=0,
                        )
                    )
            hi, lo = split(left(mat[...], jnp.concatenate(columns, axis=1)))
            for f in range(4):
                yw[f, pl.ds(G * x, G), 0:128] = hi[:, 128 * f : 128 * f + 128]
                yw[f, pl.ds(G * x, G), 128:256] = lo[:, 128 * f : 128 * f + 128]
        for f in range(4):
            p = dot(yw[f], wf[f])
            p = p[:, 0:128] + p[:, 128:256]
            if f:
                edge = 128 - 32 * f
                for x in range(XP):
                    for k in range(6):
                        r = G * x + 16 * k
                        start = 36 * count * (f - 1) + 36 * s + 6 * x + k
                        out[pl.ds(start, 16, stride=rt), :] = jnp.where(
                            lane16 < edge, held[pl.ds(r, 16), :], p[r : r + 16]
                        )
            if f < 3:
                held[...] = p


def middle_kernel(count, rec, table, mat1, mat2, out):
    rt = rows_per_dest(count)

    @pl.loop(0, count)
    def _(s):
        for kk in range(3):
            starts = [
                [36 * count * t + 36 * s + 6 * x + k for x in range(XP)]
                for k in (2 * kk, 2 * kk + 1)
                for t in range(3)
            ]
            v = jnp.concatenate(
                [
                    jnp.concatenate([rec[pl.ds(r, 16, stride=rt), :] for r in st], axis=0)
                    for st in starts
                ],
                axis=1,
            )
            v = left(mat2[...], v) * jnp.concatenate([table[2 * kk], table[2 * kk + 1]], axis=1)
            v = left(mat1[...], v)
            for i, st in enumerate(starts):
                for x in range(XP):
                    out[pl.ds(st[x], 16, stride=rt), :] = v[
                        16 * x : 16 * x + 16, 128 * i : 128 * i + 128
                    ]


def inverse_kernel(
    count, where, rec, big, image, sec, potim, mat, wi, delta, sums, phi, xw, wide, acc
):
    rt = rows_per_dest(count)
    lane = lax.broadcasted_iota(jnp.int32, (24, 128), 1)
    laneg = lax.broadcasted_iota(jnp.int32, (G, 128), 1)
    acc[...] = jnp.zeros_like(acc)

    @pl.loop(0, count)
    def _(s):
        assemble(where, big, s, phi)
        for x in range(XP):
            a, b, c = [
                jnp.concatenate(
                    [
                        rec[pl.ds(36 * count * t + 36 * s + 6 * x + k, 16, stride=rt), :]
                        for k in range(6)
                    ],
                    axis=0,
                )
                for t in range(3)
            ]
            fields = [a, jnp.where(laneg < 64, b, a), jnp.where(laneg < 32, c, b), c]
            for f in range(4):
                hi, lo = split(fields[f])
                xw[f, pl.ds(G * x, G), 0:128] = hi
                xw[f, pl.ds(G * x, G), 128:256] = lo
        for f in range(4):
            p = dot(xw[f], wi[f])
            wide[f] = p[:, 0:128] + p[:, 128:256]
        for x in range(XP):
            v = jnp.concatenate([wide[f, pl.ds(G * x, G), :] for f in range(4)], axis=1)
            v = left(mat[...], v)
            rows = [pl.ds(72 * x + 24 * b, 24) for b in range(3)]
            for n in range(OB):
                field = []
                for ri in range(2):
                    f = 2 * n + ri
                    y = [v[24 * i : 24 * i + 24, 128 * f : 128 * f + 128] for i in range(4)]
                    r1 = pltpu.roll(y[1], 96, 1)
                    r2 = pltpu.roll(y[2], 64, 1)
                    r3 = pltpu.roll(y[3], 32, 1)
                    field.append(
                        [
                            jnp.where(lane < 96, y[0], r1),
                            jnp.where(lane < 64, r1, r2),
                            jnp.where(lane < 32, r2, r3),
                        ]
                    )
                for b in range(3):
                    pr, pi = phi[0, rows[b], :], phi[1, rows[b], :]
                    vr, vi = field[0][b], field[1][b]
                    acc[0, n, rows[b], :] += pr * vr - pi * vi
                    acc[1, n, rows[b], :] += pr * vi + pi * vr

    def tail(i, carry):
        carry = list(carry)
        rows = pl.ds(pl.multiple_of(24 * i, 8), 24)
        v = potim[rows, :]
        for n in range(OB):
            re, im = image[0, n, rows, :], image[1, n, rows, :]
            sr, si = sec[0, n, rows, :], sec[1, n, rows, :]
            hr = v * sr + acc[0, n, rows, :]
            hi = v * si + acc[1, n, rows, :]
            dr = (0.5 * TIME_STEP) * (v * im + hi)
            di = (0.5 * TIME_STEP) * (-v * re - hr)
            delta[0, n, rows, :] = dr
            delta[1, n, rows, :] = di
            carry[n] = carry[n] + (re * dr + im * di)
            carry[2 + n] = carry[2 + n] + (dr * dr + di * di)
            carry[4 + n] = carry[4 + n] + (sr * hr + si * hi)
        return tuple(carry)

    zero = jnp.zeros((24, 128), F32)
    carry = lax.fori_loop(0, 18, tail, (zero,) * 6)
    rows = [jnp.sum(c, axis=0, keepdims=True) for c in carry]
    sums[...] = jnp.concatenate(rows + [jnp.zeros((2, 128), F32)], axis=0)


def stored_kernel(delta, out):
    @pl.loop(0, XP)
    def _(x):
        for c in range(2):
            for n in range(OB):
                for b in range(3):
                    rows = pl.ds(pl.multiple_of(72 * x + 24 * b, 8), 24)
                    out[pl.ds((c * XP + x) * 144 + 2 * b + n, 24, stride=6), :] = delta[
                        c, n, rows, :
                    ]


def final_kernel(gathered, psi, delta, out, total):
    t = jnp.sum(jnp.sum(gathered[...], axis=0), axis=1, keepdims=True)
    total[...] = jnp.broadcast_to(t, (8, 128))
    factor = -2.0 * t[0:2] / (t[2:4] + 1e-06)
    odd = lax.broadcasted_iota(jnp.int32, (216, 128), 0) % OB == 1
    scale = jnp.where(odd, factor[1:2], factor[0:1])

    @pl.loop(0, 8)
    def _(i):
        rows = pl.ds(pl.multiple_of(216 * i, 8), 216)
        out[rows, :] = psi[rows, :] + scale * delta[rows, :]


VM = pl.BlockSpec(memory_space=pltpu.VMEM)
SM = pl.BlockSpec(memory_space=pltpu.SMEM)


def shape(*dims):
    return jax.ShapeDtypeStruct(dims, F32)


def call(kernel, outs, ins, scratch=(), smem=0, flops=0, moved=0):
    return pl.pallas_call(
        kernel,
        out_shape=outs,
        in_specs=[SM] * smem + [VM] * (len(ins) - smem),
        out_specs=[VM] * len(outs),
        scratch_shapes=list(scratch),
        cost_estimate=pl.CostEstimate(flops=flops, bytes_accessed=moved, transcendentals=0),
    )(*ins)


def run_prepare(hi, lo):
    wide = jax.ShapeDtypeStruct((4, 256, 256), BF)
    return call(prepare_kernel, [wide, wide], [hi, lo], moved=2 << 20)


def run_section(psi, pot):
    return call(
        section_kernel,
        [shape(2, OB, 432, 128), shape(2, OB, 432, 128), shape(432, 128), shape(16, 112, 128)],
        [psi, pot],
        moved=4 << 20,
    )


def run_stored(delta):
    return call(stored_kernel, [shape(1728, 128)], [delta], moved=2 << 20)[0]


def run_final(gathered, psi, delta):
    return call(
        final_kernel, [shape(1728, 128), shape(8, 128)], [gathered, psi, delta], moved=3 << 20
    )


def run_forward(count, where, big, sec, mat, wf):
    rows = GRID * rows_per_dest(count)
    return call(
        functools.partial(forward_kernel, count),
        [shape(rows, 128)],
        [where, big, sec, mat, wf],
        [
            pltpu.VMEM((2, 432, 128), F32),
            pltpu.VMEM((4, XP * G, 256), BF),
            pltpu.VMEM((XP * G, 128), F32),
        ],
        smem=1,
        flops=count << 30,
        moved=count << 21,
    )[0]


def run_middle(count, rec, table, mat1, mat2):
    rows = GRID * rows_per_dest(count)
    return call(
        functools.partial(middle_kernel, count),
        [shape(rows, 128)],
        [rec, table, mat1, mat2],
        flops=count << 30,
        moved=count << 21,
    )[0]


def run_inverse(count, where, rec, big, image, sec, potim, mat, wi):
    return call(
        functools.partial(inverse_kernel, count),
        [shape(2, OB, 432, 128), shape(8, 128)],
        [where, rec, big, image, sec, potim, mat, wi],
        [
            pltpu.VMEM((2, 432, 128), F32),
            pltpu.VMEM((4, XP * G, 256), BF),
            pltpu.VMEM((4, XP * G, 128), F32),
            pltpu.VMEM((2, OB, 432, 128), F32),
        ],
        smem=1,
        flops=count << 30,
        moved=count << 21,
    )


def screened_table(position):
    def fold(index):
        return jnp.where(index <= G // 2, index, index - G).astype(F32)

    step = 2.0 * math.pi / BOX
    fy = fold(6 * position + jnp.arange(6, dtype=jnp.int32))[:, None, None]
    fx = fold(jnp.arange(G, dtype=jnp.int32))[None, :, None]
    fz = fold(jnp.arange(4 * G, dtype=jnp.int32) % G)[None, None, :]
    wave = (step * step) * (fx * fx + fy * fy + fz * fz)
    safe = jnp.where(wave > 0, wave, 1.0)
    screen = -jnp.expm1(-wave / (4.0 * OMEGA * OMEGA)) / safe
    screen = jnp.where(wave > 0, screen, 1.0 / (4.0 * OMEGA * OMEGA))
    return screen * (-2.0 * MIXING / (G * G * G))


RIGHT = [(h * 8 + z, h * 8 + (z + 1) % 8) for h in range(2) for z in range(8)]
LEFT = [(d, s) for s, d in RIGHT]
SWAP = [(i, i ^ 8) for i in range(16)]


def gather_sources(pieces):
    hop = lambda v, pairs: lax.ppermute(v, "band", pairs)

    def ring(v, last):
        r1, l1 = hop(v, RIGHT), hop(v, LEFT)
        r2, l2 = hop(r1, RIGHT), hop(l1, LEFT)
        r3, l3 = hop(r2, RIGHT), hop(l2, LEFT)
        far = hop(r3, RIGHT) if last else hop(l3, LEFT)
        return [v, l1, l2, l3, far, r3, r2, r1]

    own = ring(pieces, True)
    other = ring(hop(pieces, SWAP), False)
    return jnp.stack([jnp.stack(pair) for pair in zip(own, other)])


def per_device(orbitals, local_potential, plan, occupancy):
    group = jnp.arange(GROUPS, dtype=jnp.int32)
    lookup = lambda g: jnp.sum(jnp.where(group == g, occupancy, 0))
    band = lax.axis_index("band")
    where = jnp.stack([band % 8, band // 8]).astype(jnp.int32)
    (mat_fy, mat_fx, mat_ix, mat_iy), (hi, lo) = jax.tree.map(jnp.asarray, tables())
    wf, wi = run_prepare(hi, lo)
    tiled = orbitals.reshape(2, OB, XP, 72, 128).transpose(0, 2, 3, 1, 4).reshape(-1, 128)
    table = screened_table(lax.axis_index("grid"))
    sec, image, potim, pay = run_section(tiled, local_potential)
    pool = lax.all_to_all(pay, "band", 0, 0, tiled=True)
    first, second = lookup(plan[0]), lookup(plan[1])
    third = jnp.where(first > 1, plan[0], plan[1])
    slots = [(plan[0], 0), (plan[1], 0), (third, 1), (plan[1], 1)]

    def branch(count):
        def run(sec, image, potim, pool, table, wf, wi, slot_groups):
            pieces = jnp.stack(
                [
                    lax.dynamic_slice(pool, (slot_groups[i], 56 * slots[i][1], 0), (1, 56, 128))[0]
                    for i in range(count)
                ]
            )
            big = gather_sources(pieces)
            send = run_forward(count, where, big, sec, mat_fy, wf)
            got = lax.all_to_all(send, "grid", 0, 0, tiled=True)
            back = run_middle(count, got, table, mat_ix, mat_fx)
            got = lax.all_to_all(back, "grid", 0, 0, tiled=True)
            return tuple(run_inverse(count, where, got, big, image, sec, potim, mat_iy, wi))

        return run

    slot_groups = jnp.stack([g for g, _ in slots])
    delta, sums = lax.switch(
        first + second - 2,
        [branch(2), branch(3), branch(4)],
        sec,
        image,
        potim,
        pool,
        table,
        wf,
        wi,
        slot_groups,
    )
    spread = jnp.broadcast_to(sums[None], (GRID, 8, 128))
    gathered = lax.all_to_all(spread, "grid", 0, 0, tiled=True)
    fresh, total = run_final(gathered, tiled, run_stored(delta))
    fresh = fresh.reshape(2, XP, 72, OB, 128)
    fresh = fresh.transpose(0, 3, 1, 2, 4).reshape(orbitals.shape)
    own_filled = lookup(band)
    filling = jnp.where(jnp.arange(OB, dtype=jnp.int32) < own_filled, 2.0, 0.0).astype(F32)
    return (fresh, filling * total[4:6, 0] / (G * G * G))


def solution(mesh):
    return jax.shard_map(
        per_device,
        mesh=mesh,
        in_specs=(P(None, "band", "grid", None), P("grid", None), P(), P()),
        out_specs=(P(None, "band", "grid", None), P("band")),
        check_vma=False,
    )
```

```python
import functools
import math

import jax
import jax.numpy as jnp
import numpy as np
from jax import lax
from jax.experimental import pallas as pl
from jax.experimental.pallas import tpu as pltpu
from jax.sharding import PartitionSpec as P

G = 96
XP = 6
OB = 2
GROUPS = 16
GRID = 16
LANES = G * G
TIME_STEP = 0.4
MIXING = 0.25
OMEGA = 0.106
BOX = 65.1
BF = jnp.bfloat16
F32 = jnp.float32


def tables():
    index = np.arange(G)
    angle = (index[:, None] * index[None, :] % G) * (2.0 * math.pi / G)
    cas = np.cos(angle) + np.sin(angle)
    perm = np.array([6 * (i % 16) + i // 16 for i in range(G)])

    def halves(m):
        hi = np.asarray(m, np.float32).astype(jnp.bfloat16)
        lo = (m - hi.astype(np.float64)).astype(np.float32).astype(jnp.bfloat16)
        return hi, lo

    def extend(m):
        hi, lo = halves(m)
        return np.block([[hi, hi], [lo, np.zeros_like(lo)]])

    rows = np.array([4 * (i % 24) + i // 24 for i in range(G)])
    pads = [np.pad(h.astype(np.float32), (0, 128 - G)) for h in halves(cas)]
    mats = [cas[perm][:, rows], cas[:, perm], cas[perm], cas[rows][:, perm]]
    return [extend(m) for m in mats], pads


def split(v):
    hi = v.astype(BF)
    return hi, (v - hi.astype(F32)).astype(BF)


def dot(a, b):
    return jnp.dot(a, b, preferred_element_type=F32)


def left(mat, v):
    hi, lo = split(v)
    p = dot(mat, jnp.concatenate([hi, lo], axis=0))
    return p[:G] + p[G:]


def rows_per_dest(count):
    return -(-3 * 36 * count // 8) * 8


def prepare_kernel(hi, lo, wf, wi):
    zero = jnp.zeros((128, 128), BF)
    for f in range(4):
        for axis, out in ((1, wf), (0, wi)):
            shift = 96 * f % 128
            h = (pltpu.roll(hi[...], shift, axis) if shift else hi[...]).astype(BF)
            l = (pltpu.roll(lo[...], shift, axis) if shift else lo[...]).astype(BF)
            out[f, 0:128, 0:128] = h
            out[f, 128:256, 0:128] = h
            out[f, 0:128, 128:256] = l
            out[f, 128:256, 128:256] = zero


def section_kernel(psi, pot, sec, image, potim, pay):
    for t in range(72):
        a, b = t // 3, t % 3
        potim[pl.ds(24 * b + a, XP, stride=72), :] = pot[:, 128 * t : 128 * t + 128]

    @pl.loop(0, XP)
    def _(x):
        for b in range(3):
            rows = pl.ds(pl.multiple_of(72 * x + 24 * b, 8), 24)
            v = TIME_STEP * potim[rows, :]
            for n in range(OB):
                re, im = [
                    psi[pl.ds((c * XP + x) * 144 + 2 * b + n, 24, stride=6), :] for c in range(2)
                ]
                sec[0, n, rows, :] = re + v * im
                sec[1, n, rows, :] = im - v * re
                image[0, n, rows, :] = re
                image[1, n, rows, :] = im

    for c in range(2):
        for n in range(OB):
            for q in range(8):
                pay[8 * c + q, 56 * n : 56 * n + 54, :] = sec[c, n, 54 * q : 54 * q + 54, :]


def assemble(where, big, s, phi):
    for c in range(2):
        for q in range(8):
            rel = (q + 8 - where[0]) & 7
            phi[c, 54 * q : 54 * q + 54, :] = big[rel, c ^ where[1], s, 0:54, :]


def forward_kernel(count, where, big, sec, mat, wf, out, phi, yw, held):
    rt = rows_per_dest(count)
    lane = lax.broadcasted_iota(jnp.int32, (24, 128), 1)
    lane16 = lax.broadcasted_iota(jnp.int32, (16, 128), 1)

    @pl.loop(0, count)
    def _(s):
        assemble(where, big, s, phi)
        for x in range(XP):
            rows = [pl.ds(72 * x + 24 * b, 24) for b in range(3)]
            pr = [phi[0, r, :] for r in rows]
            pi = [phi[1, r, :] for r in rows]
            columns = []
            for n in range(OB):
                sr = [sec[0, n, r, :] for r in rows]
                si = [sec[1, n, r, :] for r in rows]
                for part in (
                    [pr[b] * sr[b] + pi[b] * si[b] for b in range(3)],
                    [pr[b] * si[b] - pi[b] * sr[b] for b in range(3)],
                ):
                    a, b, c = part
                    columns.append(
                        jnp.concatenate(
                            [
                                a,
                                pltpu.roll(jnp.where(lane < 96, b, a), 32, 1),
                                pltpu.roll(jnp.where(lane < 64, c, b), 64, 1),
                                pltpu.roll(c, 96, 1),
                            ],
                            axis=0,
                        )
                    )
            hi, lo = split(left(mat[...], jnp.concatenate(columns, axis=1)))
            for f in range(4):
                yw[f, pl.ds(G * x, G), 0:128] = hi[:, 128 * f : 128 * f + 128]
                yw[f, pl.ds(G * x, G), 128:256] = lo[:, 128 * f : 128 * f + 128]
        for f in range(4):
            p = dot(yw[f], wf[f])
            p = p[:, 0:128] + p[:, 128:256]
            if f:
                edge = 128 - 32 * f
                for x in range(XP):
                    for k in range(6):
                        r = G * x + 16 * k
                        start = 36 * count * (f - 1) + 36 * s + 6 * x + k
                        out[pl.ds(start, 16, stride=rt), :] = jnp.where(
                            lane16 < edge, held[pl.ds(r, 16), :], p[r : r + 16]
                        )
            if f < 3:
                held[...] = p


def middle_kernel(count, rec, table, mat1, mat2, out):
    rt = rows_per_dest(count)

    @pl.loop(0, count)
    def _(s):
        for kk in range(3):
            starts = [
                [36 * count * t + 36 * s + 6 * x + k for x in range(XP)]
                for k in (2 * kk, 2 * kk + 1)
                for t in range(3)
            ]
            v = jnp.concatenate(
                [
                    jnp.concatenate([rec[pl.ds(r, 16, stride=rt), :] for r in st], axis=0)
                    for st in starts
                ],
                axis=1,
            )
            v = left(mat2[...], v) * jnp.concatenate([table[2 * kk], table[2 * kk + 1]], axis=1)
            v = left(mat1[...], v)
            for i, st in enumerate(starts):
                for x in range(XP):
                    out[pl.ds(st[x], 16, stride=rt), :] = v[
                        16 * x : 16 * x + 16, 128 * i : 128 * i + 128
                    ]


def inverse_kernel(
    count, where, rec, big, image, sec, potim, mat, wi, delta, sums, phi, xw, wide, acc
):
    rt = rows_per_dest(count)
    lane = lax.broadcasted_iota(jnp.int32, (24, 128), 1)
    laneg = lax.broadcasted_iota(jnp.int32, (G, 128), 1)
    acc[...] = jnp.zeros_like(acc)

    @pl.loop(0, count)
    def _(s):
        assemble(where, big, s, phi)
        for x in range(XP):
            a, b, c = [
                jnp.concatenate(
                    [
                        rec[pl.ds(36 * count * t + 36 * s + 6 * x + k, 16, stride=rt), :]
                        for k in range(6)
                    ],
                    axis=0,
                )
                for t in range(3)
            ]
            fields = [a, jnp.where(laneg < 64, b, a), jnp.where(laneg < 32, c, b), c]
            for f in range(4):
                hi, lo = split(fields[f])
                xw[f, pl.ds(G * x, G), 0:128] = hi
                xw[f, pl.ds(G * x, G), 128:256] = lo
        for f in range(4):
            p = dot(xw[f], wi[f])
            wide[f] = p[:, 0:128] + p[:, 128:256]
        for x in range(XP):
            v = jnp.concatenate([wide[f, pl.ds(G * x, G), :] for f in range(4)], axis=1)
            v = left(mat[...], v)
            rows = [pl.ds(72 * x + 24 * b, 24) for b in range(3)]
            for n in range(OB):
                field = []
                for ri in range(2):
                    f = 2 * n + ri
                    y = [v[24 * i : 24 * i + 24, 128 * f : 128 * f + 128] for i in range(4)]
                    r1 = pltpu.roll(y[1], 96, 1)
                    r2 = pltpu.roll(y[2], 64, 1)
                    r3 = pltpu.roll(y[3], 32, 1)
                    field.append(
                        [
                            jnp.where(lane < 96, y[0], r1),
                            jnp.where(lane < 64, r1, r2),
                            jnp.where(lane < 32, r2, r3),
                        ]
                    )
                for b in range(3):
                    pr, pi = phi[0, rows[b], :], phi[1, rows[b], :]
                    vr, vi = field[0][b], field[1][b]
                    acc[0, n, rows[b], :] += pr * vr - pi * vi
                    acc[1, n, rows[b], :] += pr * vi + pi * vr

    def tail(i, carry):
        carry = list(carry)
        rows = pl.ds(pl.multiple_of(24 * i, 8), 24)
        v = potim[rows, :]
        for n in range(OB):
            re, im = image[0, n, rows, :], image[1, n, rows, :]
            sr, si = sec[0, n, rows, :], sec[1, n, rows, :]
            hr = v * sr + acc[0, n, rows, :]
            hi = v * si + acc[1, n, rows, :]
            dr = (0.5 * TIME_STEP) * (v * im + hi)
            di = (0.5 * TIME_STEP) * (-v * re - hr)
            delta[0, n, rows, :] = dr
            delta[1, n, rows, :] = di
            carry[n] = carry[n] + (re * dr + im * di)
            carry[2 + n] = carry[2 + n] + (dr * dr + di * di)
            carry[4 + n] = carry[4 + n] + (sr * hr + si * hi)
        return tuple(carry)

    zero = jnp.zeros((24, 128), F32)
    carry = lax.fori_loop(0, 18, tail, (zero,) * 6)
    rows = [jnp.sum(c, axis=0, keepdims=True) for c in carry]
    sums[...] = jnp.concatenate(rows + [jnp.zeros((2, 128), F32)], axis=0)


def stored_kernel(delta, out):
    @pl.loop(0, XP)
    def _(x):
        for c in range(2):
            for n in range(OB):
                for b in range(3):
                    rows = pl.ds(pl.multiple_of(72 * x + 24 * b, 8), 24)
                    out[pl.ds((c * XP + x) * 144 + 2 * b + n, 24, stride=6), :] = delta[
                        c, n, rows, :
                    ]


def final_kernel(filling, gathered, psi, delta, out, energies):
    t = jnp.sum(jnp.sum(gathered[...], axis=0), axis=1, keepdims=True)
    for n in range(OB):
        energies[n] = filling[n] * t[4 + n, 0] / (G * G * G)
    factor = -2.0 * t[0:2] / (t[2:4] + 1e-06)
    odd = lax.broadcasted_iota(jnp.int32, (216, 128), 0) % OB == 1
    scale = jnp.where(odd, factor[1:2], factor[0:1])

    @pl.loop(0, 2)
    def _(i):
        rows = pl.ds(pl.multiple_of(216 * i, 8), 216)
        out[rows, :] = psi[rows, :] + scale * delta[rows, :]


VM = pl.BlockSpec(memory_space=pltpu.VMEM)
SM = pl.BlockSpec(memory_space=pltpu.SMEM)


def shape(*dims):
    return jax.ShapeDtypeStruct(dims, F32)


def call(kernel, outs, ins, scratch=(), smem=0, flops=0, moved=0):
    return pl.pallas_call(
        kernel,
        out_shape=outs,
        in_specs=[SM] * smem + [VM] * (len(ins) - smem),
        out_specs=[VM] * len(outs),
        scratch_shapes=list(scratch),
        cost_estimate=pl.CostEstimate(flops=flops, bytes_accessed=moved, transcendentals=0),
    )(*ins)


def run_prepare(hi, lo):
    wide = jax.ShapeDtypeStruct((4, 256, 256), BF)
    return call(prepare_kernel, [wide, wide], [hi, lo], moved=2 << 20)


def run_section(psi, pot):
    return call(
        section_kernel,
        [shape(2, OB, 432, 128), shape(2, OB, 432, 128), shape(432, 128), shape(16, 112, 128)],
        [psi, pot],
        moved=4 << 20,
    )


def run_stored(delta):
    return call(stored_kernel, [shape(1728, 128)], [delta], moved=2 << 20)[0]


def run_final(filling, gathered, psi, delta):
    whole = pl.BlockSpec((GRID, 8, 128), lambda i: (0, 0, 0))
    block = pl.BlockSpec((432, 128), lambda i: (i, 0))
    return pl.pallas_call(
        final_kernel,
        out_shape=[shape(1728, 128), shape(OB)],
        grid=(4,),
        in_specs=[SM, whole, block, block],
        out_specs=[block, SM],
        cost_estimate=pl.CostEstimate(flops=1 << 20, bytes_accessed=3 << 20, transcendentals=0),
    )(filling, gathered, psi, delta)


def run_forward(count, where, big, sec, mat, wf):
    rows = GRID * rows_per_dest(count)
    return call(
        functools.partial(forward_kernel, count),
        [shape(rows, 128)],
        [where, big, sec, mat, wf],
        [
            pltpu.VMEM((2, 432, 128), F32),
            pltpu.VMEM((4, XP * G, 256), BF),
            pltpu.VMEM((XP * G, 128), F32),
        ],
        smem=1,
        flops=count << 30,
        moved=count << 21,
    )[0]


def run_middle(count, rec, table, mat1, mat2):
    rows = GRID * rows_per_dest(count)
    return call(
        functools.partial(middle_kernel, count),
        [shape(rows, 128)],
        [rec, table, mat1, mat2],
        flops=count << 30,
        moved=count << 21,
    )[0]


def run_inverse(count, where, rec, big, image, sec, potim, mat, wi):
    return call(
        functools.partial(inverse_kernel, count),
        [shape(2, OB, 432, 128), shape(8, 128)],
        [where, rec, big, image, sec, potim, mat, wi],
        [
            pltpu.VMEM((2, 432, 128), F32),
            pltpu.VMEM((4, XP * G, 256), BF),
            pltpu.VMEM((4, XP * G, 128), F32),
            pltpu.VMEM((2, OB, 432, 128), F32),
        ],
        smem=1,
        flops=count << 30,
        moved=count << 21,
    )


def screened_table(position):
    def fold(index):
        return jnp.where(index <= G // 2, index, index - G).astype(F32)

    step = 2.0 * math.pi / BOX
    fy = fold(6 * position + jnp.arange(6, dtype=jnp.int32))[:, None, None]
    fx = fold(jnp.arange(G, dtype=jnp.int32))[None, :, None]
    fz = fold(jnp.arange(4 * G, dtype=jnp.int32) % G)[None, None, :]
    wave = (step * step) * (fx * fx + fy * fy + fz * fz)
    safe = jnp.where(wave > 0, wave, 1.0)
    screen = -jnp.expm1(-wave / (4.0 * OMEGA * OMEGA)) / safe
    screen = jnp.where(wave > 0, screen, 1.0 / (4.0 * OMEGA * OMEGA))
    return screen * (-2.0 * MIXING / (G * G * G))


RIGHT = [(h * 8 + z, h * 8 + (z + 1) % 8) for h in range(2) for z in range(8)]
LEFT = [(d, s) for s, d in RIGHT]
SWAP = [(i, i ^ 8) for i in range(16)]


def gather_sources(pieces):
    hop = lambda v, pairs: lax.ppermute(v, "band", pairs)
    both = jnp.stack([pieces, hop(pieces, SWAP)])

    def step(i, carry):
        right, left, big = carry
        big = lax.dynamic_update_index_in_dim(big, left, i, 0)
        big = lax.dynamic_update_index_in_dim(big, right, (8 - i) % 8, 0)
        return hop(right, RIGHT), hop(left, LEFT), big

    big = jnp.zeros((8,) + both.shape, F32)
    _, left, big = lax.fori_loop(0, 4, step, (both, both, big))
    return lax.dynamic_update_index_in_dim(big, left, 4, 0)


def per_device(orbitals, local_potential, plan, occupancy):
    group = jnp.arange(GROUPS, dtype=jnp.int32)
    lookup = lambda g: jnp.sum(jnp.where(group == g, occupancy, 0))
    band = lax.axis_index("band")
    where = jnp.stack([band % 8, band // 8]).astype(jnp.int32)
    (mat_fy, mat_fx, mat_ix, mat_iy), (hi, lo) = jax.tree.map(jnp.asarray, tables())
    wf, wi = run_prepare(hi, lo)
    tiled = orbitals.reshape(2, OB, XP, 72, 128).transpose(0, 2, 3, 1, 4).reshape(-1, 128)
    table = screened_table(lax.axis_index("grid"))
    sec, image, potim, pay = run_section(tiled, local_potential)
    pool = lax.all_to_all(pay, "band", 0, 0, tiled=True)
    first, second = lookup(plan[0]), lookup(plan[1])
    third = jnp.where(first > 1, plan[0], plan[1])
    slots = [(plan[0], 0), (plan[1], 0), (third, 1), (plan[1], 1)]

    def branch(count):
        def run(sec, image, potim, pool, table, wf, wi, slot_groups):
            pieces = jnp.stack(
                [
                    lax.dynamic_slice(pool, (slot_groups[i], 56 * slots[i][1], 0), (1, 56, 128))[0]
                    for i in range(count)
                ]
            )
            big = gather_sources(pieces)
            send = run_forward(count, where, big, sec, mat_fy, wf)
            got = lax.all_to_all(send, "grid", 0, 0, tiled=True)
            back = run_middle(count, got, table, mat_ix, mat_fx)
            got = lax.all_to_all(back, "grid", 0, 0, tiled=True)
            return tuple(run_inverse(count, where, got, big, image, sec, potim, mat_iy, wi))

        return run

    slot_groups = jnp.stack([g for g, _ in slots])
    delta, sums = lax.switch(
        first + second - 2,
        [branch(2), branch(3), branch(4)],
        sec,
        image,
        potim,
        pool,
        table,
        wf,
        wi,
        slot_groups,
    )
    spread = jnp.broadcast_to(sums[None], (GRID, 8, 128))
    gathered = lax.all_to_all(spread, "grid", 0, 0, tiled=True)
    own_filled = lookup(band)
    filling = jnp.where(jnp.arange(OB, dtype=jnp.int32) < own_filled, 2.0, 0.0).astype(F32)
    fresh, energies = run_final(filling, gathered, tiled, run_stored(delta))
    fresh = fresh.reshape(2, XP, 72, OB, 128)
    fresh = fresh.transpose(0, 3, 1, 2, 4).reshape(orbitals.shape)
    return (fresh, energies)


def solution(mesh):
    return jax.shard_map(
        per_device,
        mesh=mesh,
        in_specs=(P(None, "band", "grid", None), P("grid", None), P(), P()),
        out_specs=(P(None, "band", "grid", None), P("band")),
        check_vma=False,
    )
```

```python
import functools
import math

import jax
import jax.numpy as jnp
import numpy as np
from jax import lax
from jax.experimental import pallas as pl
from jax.experimental.pallas import tpu as pltpu
from jax.sharding import PartitionSpec as P

G = 96
XP = 6
OB = 2
GROUPS = 16
GRID = 16
LANES = G * G
TIME_STEP = 0.4
MIXING = 0.25
OMEGA = 0.106
BOX = 65.1
BF = jnp.bfloat16
F32 = jnp.float32


def tables():
    index = np.arange(G)
    angle = (index[:, None] * index[None, :] % G) * (2.0 * math.pi / G)
    cas = np.cos(angle) + np.sin(angle)
    perm = np.array([6 * (i % 16) + i // 16 for i in range(G)])

    def halves(m):
        hi = np.asarray(m, np.float32).astype(jnp.bfloat16)
        lo = (m - hi.astype(np.float64)).astype(np.float32).astype(jnp.bfloat16)
        return hi, lo

    def extend(m):
        hi, lo = halves(m)
        return np.block([[hi, hi], [lo, np.zeros_like(lo)]])

    rows = np.array([4 * (i % 24) + i // 24 for i in range(G)])
    pads = [np.pad(h.astype(np.float32), (0, 128 - G)) for h in halves(cas)]
    mats = [cas[perm][:, rows], cas[:, perm], cas[perm], cas[rows][:, perm]]
    return [extend(m) for m in mats], pads


def split(v):
    hi = v.astype(BF)
    return hi, (v - hi.astype(F32)).astype(BF)


def dot(a, b):
    return jnp.dot(a, b, preferred_element_type=F32)


def left(mat, v):
    hi, lo = split(v)
    p = dot(mat, jnp.concatenate([hi, lo], axis=0))
    return p[:G] + p[G:]


def rows_per_dest(count):
    return -(-3 * 36 * count // 8) * 8


def prepare_kernel(hi, lo, wf, wi):
    zero = jnp.zeros((128, 128), BF)
    for f in range(4):
        for axis, out in ((1, wf), (0, wi)):
            shift = 96 * f % 128
            h = (pltpu.roll(hi[...], shift, axis) if shift else hi[...]).astype(BF)
            l = (pltpu.roll(lo[...], shift, axis) if shift else lo[...]).astype(BF)
            out[f, 0:128, 0:128] = h
            out[f, 128:256, 0:128] = h
            out[f, 0:128, 128:256] = l
            out[f, 128:256, 128:256] = zero


def section_kernel(psi, pot, sec, image, potim, pay):
    for t in range(72):
        a, b = t // 3, t % 3
        potim[pl.ds(24 * b + a, XP, stride=72), :] = pot[:, 128 * t : 128 * t + 128]

    @pl.loop(0, XP)
    def _(x):
        for b in range(3):
            rows = pl.ds(pl.multiple_of(72 * x + 24 * b, 8), 24)
            v = TIME_STEP * potim[rows, :]
            for n in range(OB):
                re, im = [
                    psi[pl.ds((c * XP + x) * 144 + 2 * b + n, 24, stride=6), :] for c in range(2)
                ]
                sec[0, n, rows, :] = re + v * im
                sec[1, n, rows, :] = im - v * re
                image[0, n, rows, :] = re
                image[1, n, rows, :] = im

    for c in range(2):
        for n in range(OB):
            for q in range(8):
                pay[8 * c + q, 56 * n : 56 * n + 54, :] = sec[c, n, 54 * q : 54 * q + 54, :]


def assemble(where, big, s, phi):
    for c in range(2):
        for q in range(8):
            rel = (q + 8 - where[0]) & 7
            phi[c, 54 * q : 54 * q + 54, :] = big[rel, c ^ where[1], s, 0:54, :]


def forward_kernel(count, where, big, sec, mat, wf, out, phi, yw, held):
    rt = rows_per_dest(count)
    lane = lax.broadcasted_iota(jnp.int32, (24, 128), 1)
    lane16 = lax.broadcasted_iota(jnp.int32, (16, 128), 1)

    @pl.loop(0, count)
    def _(s):
        assemble(where, big, s, phi)
        for x in range(XP):
            rows = [pl.ds(72 * x + 24 * b, 24) for b in range(3)]
            pr = [phi[0, r, :] for r in rows]
            pi = [phi[1, r, :] for r in rows]
            columns = []
            for n in range(OB):
                sr = [sec[0, n, r, :] for r in rows]
                si = [sec[1, n, r, :] for r in rows]
                for part in (
                    [pr[b] * sr[b] + pi[b] * si[b] for b in range(3)],
                    [pr[b] * si[b] - pi[b] * sr[b] for b in range(3)],
                ):
                    a, b, c = part
                    columns.append(
                        jnp.concatenate(
                            [
                                a,
                                pltpu.roll(jnp.where(lane < 96, b, a), 32, 1),
                                pltpu.roll(jnp.where(lane < 64, c, b), 64, 1),
                                pltpu.roll(c, 96, 1),
                            ],
                            axis=0,
                        )
                    )
            hi, lo = split(left(mat[...], jnp.concatenate(columns, axis=1)))
            for f in range(4):
                yw[f, pl.ds(G * x, G), 0:128] = hi[:, 128 * f : 128 * f + 128]
                yw[f, pl.ds(G * x, G), 128:256] = lo[:, 128 * f : 128 * f + 128]
        for f in range(4):
            p = dot(yw[f], wf[f])
            p = p[:, 0:128] + p[:, 128:256]
            if f:
                edge = 128 - 32 * f
                for x in range(XP):
                    for k in range(6):
                        r = G * x + 16 * k
                        start = 36 * count * (f - 1) + 36 * s + 6 * x + k
                        out[pl.ds(start, 16, stride=rt), :] = jnp.where(
                            lane16 < edge, held[pl.ds(r, 16), :], p[r : r + 16]
                        )
            if f < 3:
                held[...] = p


def middle_kernel(count, rec, table, mat1, mat2, out):
    rt = rows_per_dest(count)

    @pl.loop(0, count)
    def _(s):
        for kk in range(3):
            starts = [
                [36 * count * t + 36 * s + 6 * x + k for x in range(XP)]
                for k in (2 * kk, 2 * kk + 1)
                for t in range(3)
            ]
            v = jnp.concatenate(
                [
                    jnp.concatenate([rec[pl.ds(r, 16, stride=rt), :] for r in st], axis=0)
                    for st in starts
                ],
                axis=1,
            )
            v = left(mat2[...], v) * jnp.concatenate([table[2 * kk], table[2 * kk + 1]], axis=1)
            v = left(mat1[...], v)
            for i, st in enumerate(starts):
                for x in range(XP):
                    out[pl.ds(st[x], 16, stride=rt), :] = v[
                        16 * x : 16 * x + 16, 128 * i : 128 * i + 128
                    ]


def inverse_kernel(
    count, where, rec, big, image, sec, potim, mat, wi, delta, sums, phi, xw, wide, acc
):
    rt = rows_per_dest(count)
    lane = lax.broadcasted_iota(jnp.int32, (24, 128), 1)
    laneg = lax.broadcasted_iota(jnp.int32, (G, 128), 1)
    acc[...] = jnp.zeros_like(acc)

    @pl.loop(0, count)
    def _(s):
        assemble(where, big, s, phi)
        for x in range(XP):
            a, b, c = [
                jnp.concatenate(
                    [
                        rec[pl.ds(36 * count * t + 36 * s + 6 * x + k, 16, stride=rt), :]
                        for k in range(6)
                    ],
                    axis=0,
                )
                for t in range(3)
            ]
            fields = [a, jnp.where(laneg < 64, b, a), jnp.where(laneg < 32, c, b), c]
            for f in range(4):
                hi, lo = split(fields[f])
                xw[f, pl.ds(G * x, G), 0:128] = hi
                xw[f, pl.ds(G * x, G), 128:256] = lo
        for f in range(4):
            p = dot(xw[f], wi[f])
            wide[f] = p[:, 0:128] + p[:, 128:256]
        for x in range(XP):
            v = jnp.concatenate([wide[f, pl.ds(G * x, G), :] for f in range(4)], axis=1)
            v = left(mat[...], v)
            rows = [pl.ds(72 * x + 24 * b, 24) for b in range(3)]
            for n in range(OB):
                field = []
                for ri in range(2):
                    f = 2 * n + ri
                    y = [v[24 * i : 24 * i + 24, 128 * f : 128 * f + 128] for i in range(4)]
                    r1 = pltpu.roll(y[1], 96, 1)
                    r2 = pltpu.roll(y[2], 64, 1)
                    r3 = pltpu.roll(y[3], 32, 1)
                    field.append(
                        [
                            jnp.where(lane < 96, y[0], r1),
                            jnp.where(lane < 64, r1, r2),
                            jnp.where(lane < 32, r2, r3),
                        ]
                    )
                for b in range(3):
                    pr, pi = phi[0, rows[b], :], phi[1, rows[b], :]
                    vr, vi = field[0][b], field[1][b]
                    acc[0, n, rows[b], :] += pr * vr - pi * vi
                    acc[1, n, rows[b], :] += pr * vi + pi * vr

    def tail(i, carry):
        carry = list(carry)
        rows = pl.ds(pl.multiple_of(24 * i, 8), 24)
        v = potim[rows, :]
        for n in range(OB):
            re, im = image[0, n, rows, :], image[1, n, rows, :]
            sr, si = sec[0, n, rows, :], sec[1, n, rows, :]
            hr = v * sr + acc[0, n, rows, :]
            hi = v * si + acc[1, n, rows, :]
            dr = (0.5 * TIME_STEP) * (v * im + hi)
            di = (0.5 * TIME_STEP) * (-v * re - hr)
            delta[0, n, rows, :] = dr
            delta[1, n, rows, :] = di
            carry[n] = carry[n] + (re * dr + im * di)
            carry[2 + n] = carry[2 + n] + (dr * dr + di * di)
            carry[4 + n] = carry[4 + n] + (sr * hr + si * hi)
        return tuple(carry)

    zero = jnp.zeros((24, 128), F32)
    carry = lax.fori_loop(0, 18, tail, (zero,) * 6)
    rows = [jnp.sum(c, axis=0, keepdims=True) for c in carry]
    sums[...] = jnp.concatenate(rows + [jnp.zeros((2, 128), F32)], axis=0)


def stored_kernel(delta, out):
    @pl.loop(0, XP)
    def _(x):
        for c in range(2):
            for n in range(OB):
                for b in range(3):
                    rows = pl.ds(pl.multiple_of(72 * x + 24 * b, 8), 24)
                    out[pl.ds((c * XP + x) * 144 + 2 * b + n, 24, stride=6), :] = delta[
                        c, n, rows, :
                    ]


def final_kernel(filling, gathered, psi, delta, out, energies):
    t = jnp.sum(jnp.sum(gathered[...], axis=0), axis=1, keepdims=True)
    factor = -2.0 * t[0:2] / (t[2:4] + 1e-06)
    odd = lax.broadcasted_iota(jnp.int32, (216, 128), 0) % OB == 1
    scale = jnp.where(odd, factor[1:2], factor[0:1])

    @pl.loop(0, 8)
    def _(i):
        rows = pl.ds(pl.multiple_of(216 * i, 8), 216)
        out[rows, :] = psi[rows, :] + scale * delta[rows, :]

    for n in range(OB):
        energies[n] = filling[n] * t[4 + n, 0] / (G * G * G)


VM = pl.BlockSpec(memory_space=pltpu.VMEM)
SM = pl.BlockSpec(memory_space=pltpu.SMEM)


def shape(*dims):
    return jax.ShapeDtypeStruct(dims, F32)


def call(kernel, outs, ins, scratch=(), smem=0, flops=0, moved=0):
    return pl.pallas_call(
        kernel,
        out_shape=outs,
        in_specs=[SM] * smem + [VM] * (len(ins) - smem),
        out_specs=[VM] * len(outs),
        scratch_shapes=list(scratch),
        cost_estimate=pl.CostEstimate(flops=flops, bytes_accessed=moved, transcendentals=0),
    )(*ins)


def run_prepare(hi, lo):
    wide = jax.ShapeDtypeStruct((4, 256, 256), BF)
    return call(prepare_kernel, [wide, wide], [hi, lo], moved=2 << 20)


def run_section(psi, pot):
    return call(
        section_kernel,
        [shape(2, OB, 432, 128), shape(2, OB, 432, 128), shape(432, 128), shape(16, 112, 128)],
        [psi, pot],
        moved=4 << 20,
    )


def run_stored(delta):
    return call(stored_kernel, [shape(1728, 128)], [delta], moved=2 << 20)[0]


def run_final(filling, gathered, psi, delta):
    return pl.pallas_call(
        final_kernel,
        out_shape=[shape(1728, 128), shape(OB)],
        in_specs=[SM, VM, VM, VM],
        out_specs=[VM, SM],
        cost_estimate=pl.CostEstimate(flops=1 << 20, bytes_accessed=3 << 20, transcendentals=0),
    )(filling, gathered, psi, delta)


def run_forward(count, where, big, sec, mat, wf):
    rows = GRID * rows_per_dest(count)
    return call(
        functools.partial(forward_kernel, count),
        [shape(rows, 128)],
        [where, big, sec, mat, wf],
        [
            pltpu.VMEM((2, 432, 128), F32),
            pltpu.VMEM((4, XP * G, 256), BF),
            pltpu.VMEM((XP * G, 128), F32),
        ],
        smem=1,
        flops=count << 30,
        moved=count << 21,
    )[0]


def run_middle(count, rec, table, mat1, mat2):
    rows = GRID * rows_per_dest(count)
    return call(
        functools.partial(middle_kernel, count),
        [shape(rows, 128)],
        [rec, table, mat1, mat2],
        flops=count << 30,
        moved=count << 21,
    )[0]


def run_inverse(count, where, rec, big, image, sec, potim, mat, wi):
    return call(
        functools.partial(inverse_kernel, count),
        [shape(2, OB, 432, 128), shape(8, 128)],
        [where, rec, big, image, sec, potim, mat, wi],
        [
            pltpu.VMEM((2, 432, 128), F32),
            pltpu.VMEM((4, XP * G, 256), BF),
            pltpu.VMEM((4, XP * G, 128), F32),
            pltpu.VMEM((2, OB, 432, 128), F32),
        ],
        smem=1,
        flops=count << 30,
        moved=count << 21,
    )


def screened_table(position):
    def fold(index):
        return jnp.where(index <= G // 2, index, index - G).astype(F32)

    step = 2.0 * math.pi / BOX
    fy = fold(6 * position + jnp.arange(6, dtype=jnp.int32))[:, None, None]
    fx = fold(jnp.arange(G, dtype=jnp.int32))[None, :, None]
    fz = fold(jnp.arange(4 * G, dtype=jnp.int32) % G)[None, None, :]
    wave = (step * step) * (fx * fx + fy * fy + fz * fz)
    safe = jnp.where(wave > 0, wave, 1.0)
    screen = -jnp.expm1(-wave / (4.0 * OMEGA * OMEGA)) / safe
    screen = jnp.where(wave > 0, screen, 1.0 / (4.0 * OMEGA * OMEGA))
    return screen * (-2.0 * MIXING / (G * G * G))


RIGHT = [(h * 8 + z, h * 8 + (z + 1) % 8) for h in range(2) for z in range(8)]
LEFT = [(d, s) for s, d in RIGHT]
SWAP = [(i, i ^ 8) for i in range(16)]


def gather_sources(pieces):
    hop = lambda v, pairs: lax.ppermute(v, "band", pairs)
    both = jnp.stack([pieces, hop(pieces, SWAP)])

    def step(i, carry):
        right, left, big = carry
        big = lax.dynamic_update_index_in_dim(big, left, i, 0)
        big = lax.dynamic_update_index_in_dim(big, right, (8 - i) % 8, 0)
        return hop(right, RIGHT), hop(left, LEFT), big

    big = jnp.zeros((8,) + both.shape, F32)
    _, left, big = lax.fori_loop(0, 4, step, (both, both, big))
    return lax.dynamic_update_index_in_dim(big, left, 4, 0)


def per_device(orbitals, local_potential, plan, occupancy):
    group = jnp.arange(GROUPS, dtype=jnp.int32)
    lookup = lambda g: jnp.sum(jnp.where(group == g, occupancy, 0))
    band = lax.axis_index("band")
    where = jnp.stack([band % 8, band // 8]).astype(jnp.int32)
    (mat_fy, mat_fx, mat_ix, mat_iy), (hi, lo) = jax.tree.map(jnp.asarray, tables())
    wf, wi = run_prepare(hi, lo)
    tiled = orbitals.reshape(2, OB, XP, 72, 128).transpose(0, 2, 3, 1, 4).reshape(-1, 128)
    table = screened_table(lax.axis_index("grid"))
    sec, image, potim, pay = run_section(tiled, local_potential)
    pool = lax.all_to_all(pay, "band", 0, 0, tiled=True)
    first, second = lookup(plan[0]), lookup(plan[1])
    third = jnp.where(first > 1, plan[0], plan[1])
    slots = [(plan[0], 0), (plan[1], 0), (third, 1), (plan[1], 1)]
    chosen = jnp.stack(
        [lax.dynamic_slice(pool, (g, 56 * j, 0), (1, 56, 128))[0] for g, j in slots]
    )

    def branch(count):
        def run(sec, image, potim, chosen, table, wf, wi):
            pieces = chosen[:count]
            big = gather_sources(pieces)
            send = run_forward(count, where, big, sec, mat_fy, wf)
            got = lax.all_to_all(send, "grid", 0, 0, tiled=True)
            back = run_middle(count, got, table, mat_ix, mat_fx)
            got = lax.all_to_all(back, "grid", 0, 0, tiled=True)
            return tuple(run_inverse(count, where, got, big, image, sec, potim, mat_iy, wi))

        return run

    delta, sums = lax.switch(
        first + second - 2,
        [branch(2), branch(3), branch(4)],
        sec,
        image,
        potim,
        chosen,
        table,
        wf,
        wi,
    )
    spread = jnp.broadcast_to(sums[None], (GRID, 8, 128))
    gathered = lax.all_to_all(spread, "grid", 0, 0, tiled=True)
    own_filled = lookup(band)
    filling = jnp.where(jnp.arange(OB, dtype=jnp.int32) < own_filled, 2.0, 0.0).astype(F32)
    fresh, energies = run_final(filling, gathered, tiled, run_stored(delta))
    fresh = fresh.reshape(2, XP, 72, OB, 128)
    fresh = fresh.transpose(0, 3, 1, 2, 4).reshape(orbitals.shape)
    return (fresh, energies)


def solution(mesh):
    return jax.shard_map(
        per_device,
        mesh=mesh,
        in_specs=(P(None, "band", "grid", None), P("grid", None), P(), P()),
        out_specs=(P(None, "band", "grid", None), P("band")),
        check_vma=False,
    )
```

```python
import functools
import math

import jax
import jax.numpy as jnp
import numpy as np
from jax import lax
from jax.experimental import pallas as pl
from jax.experimental.pallas import tpu as pltpu
from jax.sharding import PartitionSpec as P

G = 96
XP = 6
OB = 2
GROUPS = 16
GRID = 16
LANES = G * G
TIME_STEP = 0.4
MIXING = 0.25
OMEGA = 0.106
BOX = 65.1
BF = jnp.bfloat16
F32 = jnp.float32


def tables():
    index = np.arange(G)
    angle = (index[:, None] * index[None, :] % G) * (2.0 * math.pi / G)
    cas = np.cos(angle) + np.sin(angle)
    perm = np.array([6 * (i % 16) + i // 16 for i in range(G)])

    def halves(m):
        hi = np.asarray(m, np.float32).astype(jnp.bfloat16)
        lo = (m - hi.astype(np.float64)).astype(np.float32).astype(jnp.bfloat16)
        return hi, lo

    def extend(m):
        hi, lo = halves(m)
        return np.block([[hi, hi], [lo, np.zeros_like(lo)]])

    rows = np.array([4 * (i % 24) + i // 24 for i in range(G)])
    pads = [np.pad(h.astype(np.float32), (0, 128 - G)) for h in halves(cas)]
    mats = [cas[perm][:, rows], cas[:, perm], cas[perm], cas[rows][:, perm]]
    return [extend(m) for m in mats], pads


def split(v):
    hi = v.astype(BF)
    return hi, (v - hi.astype(F32)).astype(BF)


def dot(a, b):
    return jnp.dot(a, b, preferred_element_type=F32)


def left(mat, v):
    hi, lo = split(v)
    p = dot(mat, jnp.concatenate([hi, lo], axis=0))
    return p[:G] + p[G:]


def rows_per_dest(count):
    return -(-3 * 36 * count // 8) * 8


def prepare_kernel(hi, lo, wf, wi):
    zero = jnp.zeros((128, 128), BF)
    for f in range(4):
        for axis, out in ((1, wf), (0, wi)):
            shift = 96 * f % 128
            h = (pltpu.roll(hi[...], shift, axis) if shift else hi[...]).astype(BF)
            l = (pltpu.roll(lo[...], shift, axis) if shift else lo[...]).astype(BF)
            out[f, 0:128, 0:128] = h
            out[f, 128:256, 0:128] = h
            out[f, 0:128, 128:256] = l
            out[f, 128:256, 128:256] = zero


def section_kernel(psi, pot, sec, image, potim, pay):
    for t in range(72):
        a, b = t // 3, t % 3
        potim[pl.ds(24 * b + a, XP, stride=72), :] = pot[:, 128 * t : 128 * t + 128]

    @pl.loop(0, XP)
    def _(x):
        for b in range(3):
            rows = pl.ds(pl.multiple_of(72 * x + 24 * b, 8), 24)
            v = TIME_STEP * potim[rows, :]
            for n in range(OB):
                re, im = [
                    psi[pl.ds((c * XP + x) * 144 + 2 * b + n, 24, stride=6), :] for c in range(2)
                ]
                sec[0, n, rows, :] = re + v * im
                sec[1, n, rows, :] = im - v * re
                image[0, n, rows, :] = re
                image[1, n, rows, :] = im

    for c in range(2):
        for n in range(OB):
            for q in range(8):
                r = 56 * (2 * n + c)
                pay[q, r : r + 54, :] = sec[c, n, 54 * q : 54 * q + 54, :]


def assemble(where, big, s, phi):
    for c in range(2):
        for q in range(8):
            rel = (q + 8 - where[0]) & 7
            phi[c, 54 * q : 54 * q + 54, :] = big[rel, s, c, 0:54, :]


def forward_kernel(count, where, big, sec, mat, wf, out, phi, yw, held):
    rt = rows_per_dest(count)
    lane = lax.broadcasted_iota(jnp.int32, (24, 128), 1)
    lane16 = lax.broadcasted_iota(jnp.int32, (16, 128), 1)

    @pl.loop(0, count)
    def _(s):
        assemble(where, big, s, phi)
        for x in range(XP):
            rows = [pl.ds(72 * x + 24 * b, 24) for b in range(3)]
            pr = [phi[0, r, :] for r in rows]
            pi = [phi[1, r, :] for r in rows]
            columns = []
            for n in range(OB):
                sr = [sec[0, n, r, :] for r in rows]
                si = [sec[1, n, r, :] for r in rows]
                for part in (
                    [pr[b] * sr[b] + pi[b] * si[b] for b in range(3)],
                    [pr[b] * si[b] - pi[b] * sr[b] for b in range(3)],
                ):
                    a, b, c = part
                    columns.append(
                        jnp.concatenate(
                            [
                                a,
                                pltpu.roll(jnp.where(lane < 96, b, a), 32, 1),
                                pltpu.roll(jnp.where(lane < 64, c, b), 64, 1),
                                pltpu.roll(c, 96, 1),
                            ],
                            axis=0,
                        )
                    )
            hi, lo = split(left(mat[...], jnp.concatenate(columns, axis=1)))
            for f in range(4):
                yw[f, pl.ds(G * x, G), 0:128] = hi[:, 128 * f : 128 * f + 128]
                yw[f, pl.ds(G * x, G), 128:256] = lo[:, 128 * f : 128 * f + 128]
        for f in range(4):
            p = dot(yw[f], wf[f])
            p = p[:, 0:128] + p[:, 128:256]
            if f:
                edge = 128 - 32 * f
                for x in range(XP):
                    for k in range(6):
                        r = G * x + 16 * k
                        start = 36 * count * (f - 1) + 36 * s + 6 * x + k
                        out[pl.ds(start, 16, stride=rt), :] = jnp.where(
                            lane16 < edge, held[pl.ds(r, 16), :], p[r : r + 16]
                        )
            if f < 3:
                held[...] = p


def middle_kernel(count, rec, table, mat1, mat2, out):
    rt = rows_per_dest(count)

    @pl.loop(0, count)
    def _(s):
        for kk in range(3):
            starts = [
                [36 * count * t + 36 * s + 6 * x + k for x in range(XP)]
                for k in (2 * kk, 2 * kk + 1)
                for t in range(3)
            ]
            v = jnp.concatenate(
                [
                    jnp.concatenate([rec[pl.ds(r, 16, stride=rt), :] for r in st], axis=0)
                    for st in starts
                ],
                axis=1,
            )
            v = left(mat2[...], v) * jnp.concatenate([table[2 * kk], table[2 * kk + 1]], axis=1)
            v = left(mat1[...], v)
            for i, st in enumerate(starts):
                for x in range(XP):
                    out[pl.ds(st[x], 16, stride=rt), :] = v[
                        16 * x : 16 * x + 16, 128 * i : 128 * i + 128
                    ]


def inverse_kernel(
    count, where, rec, big, image, sec, potim, mat, wi, delta, sums, phi, xw, wide, acc
):
    rt = rows_per_dest(count)
    lane = lax.broadcasted_iota(jnp.int32, (24, 128), 1)
    laneg = lax.broadcasted_iota(jnp.int32, (G, 128), 1)
    acc[...] = jnp.zeros_like(acc)

    @pl.loop(0, count)
    def _(s):
        assemble(where, big, s, phi)
        for x in range(XP):
            a, b, c = [
                jnp.concatenate(
                    [
                        rec[pl.ds(36 * count * t + 36 * s + 6 * x + k, 16, stride=rt), :]
                        for k in range(6)
                    ],
                    axis=0,
                )
                for t in range(3)
            ]
            fields = [a, jnp.where(laneg < 64, b, a), jnp.where(laneg < 32, c, b), c]
            for f in range(4):
                hi, lo = split(fields[f])
                xw[f, pl.ds(G * x, G), 0:128] = hi
                xw[f, pl.ds(G * x, G), 128:256] = lo
        for f in range(4):
            p = dot(xw[f], wi[f])
            wide[f] = p[:, 0:128] + p[:, 128:256]
        for x in range(XP):
            v = jnp.concatenate([wide[f, pl.ds(G * x, G), :] for f in range(4)], axis=1)
            v = left(mat[...], v)
            rows = [pl.ds(72 * x + 24 * b, 24) for b in range(3)]
            for n in range(OB):
                field = []
                for ri in range(2):
                    f = 2 * n + ri
                    y = [v[24 * i : 24 * i + 24, 128 * f : 128 * f + 128] for i in range(4)]
                    r1 = pltpu.roll(y[1], 96, 1)
                    r2 = pltpu.roll(y[2], 64, 1)
                    r3 = pltpu.roll(y[3], 32, 1)
                    field.append(
                        [
                            jnp.where(lane < 96, y[0], r1),
                            jnp.where(lane < 64, r1, r2),
                            jnp.where(lane < 32, r2, r3),
                        ]
                    )
                for b in range(3):
                    pr, pi = phi[0, rows[b], :], phi[1, rows[b], :]
                    vr, vi = field[0][b], field[1][b]
                    acc[0, n, rows[b], :] += pr * vr - pi * vi
                    acc[1, n, rows[b], :] += pr * vi + pi * vr

    def tail(i, carry):
        carry = list(carry)
        rows = pl.ds(pl.multiple_of(24 * i, 8), 24)
        v = potim[rows, :]
        for n in range(OB):
            re, im = image[0, n, rows, :], image[1, n, rows, :]
            sr, si = sec[0, n, rows, :], sec[1, n, rows, :]
            hr = v * sr + acc[0, n, rows, :]
            hi = v * si + acc[1, n, rows, :]
            dr = (0.5 * TIME_STEP) * (v * im + hi)
            di = (0.5 * TIME_STEP) * (-v * re - hr)
            delta[0, n, rows, :] = dr
            delta[1, n, rows, :] = di
            carry[n] = carry[n] + (re * dr + im * di)
            carry[2 + n] = carry[2 + n] + (dr * dr + di * di)
            carry[4 + n] = carry[4 + n] + (sr * hr + si * hi)
        return tuple(carry)

    zero = jnp.zeros((24, 128), F32)
    carry = lax.fori_loop(0, 18, tail, (zero,) * 6)
    rows = [jnp.sum(c, axis=0, keepdims=True) for c in carry]
    sums[...] = jnp.concatenate(rows + [jnp.zeros((2, 128), F32)], axis=0)


def stored_kernel(delta, out):
    @pl.loop(0, XP)
    def _(x):
        for c in range(2):
            for n in range(OB):
                for b in range(3):
                    rows = pl.ds(pl.multiple_of(72 * x + 24 * b, 8), 24)
                    out[pl.ds((c * XP + x) * 144 + 2 * b + n, 24, stride=6), :] = delta[
                        c, n, rows, :
                    ]


def final_kernel(filling, gathered, psi, delta, out, energies):
    t = jnp.sum(jnp.sum(gathered[...], axis=0), axis=1, keepdims=True)
    factor = -2.0 * t[0:2] / (t[2:4] + 1e-06)
    odd = lax.broadcasted_iota(jnp.int32, (216, 128), 0) % OB == 1
    scale = jnp.where(odd, factor[1:2], factor[0:1])

    @pl.loop(0, 8)
    def _(i):
        rows = pl.ds(pl.multiple_of(216 * i, 8), 216)
        out[rows, :] = psi[rows, :] + scale * delta[rows, :]

    for n in range(OB):
        energies[n] = filling[n] * t[4 + n, 0] / (G * G * G)


VM = pl.BlockSpec(memory_space=pltpu.VMEM)
SM = pl.BlockSpec(memory_space=pltpu.SMEM)


def shape(*dims):
    return jax.ShapeDtypeStruct(dims, F32)


def call(kernel, outs, ins, scratch=(), smem=0, flops=0, moved=0):
    return pl.pallas_call(
        kernel,
        out_shape=outs,
        in_specs=[SM] * smem + [VM] * (len(ins) - smem),
        out_specs=[VM] * len(outs),
        scratch_shapes=list(scratch),
        cost_estimate=pl.CostEstimate(flops=flops, bytes_accessed=moved, transcendentals=0),
    )(*ins)


def run_prepare(hi, lo):
    wide = jax.ShapeDtypeStruct((4, 256, 256), BF)
    return call(prepare_kernel, [wide, wide], [hi, lo], moved=2 << 20)


def run_section(psi, pot):
    return call(
        section_kernel,
        [shape(2, OB, 432, 128), shape(2, OB, 432, 128), shape(432, 128), shape(8, 224, 128)],
        [psi, pot],
        moved=4 << 20,
    )


def run_stored(delta):
    return call(stored_kernel, [shape(1728, 128)], [delta], moved=2 << 20)[0]


def run_final(filling, gathered, psi, delta):
    return pl.pallas_call(
        final_kernel,
        out_shape=[shape(1728, 128), shape(OB)],
        in_specs=[SM, VM, VM, VM],
        out_specs=[VM, SM],
        cost_estimate=pl.CostEstimate(flops=1 << 20, bytes_accessed=3 << 20, transcendentals=0),
    )(filling, gathered, psi, delta)


def run_forward(count, where, big, sec, mat, wf):
    rows = GRID * rows_per_dest(count)
    return call(
        functools.partial(forward_kernel, count),
        [shape(rows, 128)],
        [where, big, sec, mat, wf],
        [
            pltpu.VMEM((2, 432, 128), F32),
            pltpu.VMEM((4, XP * G, 256), BF),
            pltpu.VMEM((XP * G, 128), F32),
        ],
        smem=1,
        flops=count << 30,
        moved=count << 21,
    )[0]


def run_middle(count, rec, table, mat1, mat2):
    rows = GRID * rows_per_dest(count)
    return call(
        functools.partial(middle_kernel, count),
        [shape(rows, 128)],
        [rec, table, mat1, mat2],
        flops=count << 30,
        moved=count << 21,
    )[0]


def run_inverse(count, where, rec, big, image, sec, potim, mat, wi):
    return call(
        functools.partial(inverse_kernel, count),
        [shape(2, OB, 432, 128), shape(8, 128)],
        [where, rec, big, image, sec, potim, mat, wi],
        [
            pltpu.VMEM((2, 432, 128), F32),
            pltpu.VMEM((4, XP * G, 256), BF),
            pltpu.VMEM((4, XP * G, 128), F32),
            pltpu.VMEM((2, OB, 432, 128), F32),
        ],
        smem=1,
        flops=count << 30,
        moved=count << 21,
    )


def screened_table(position):
    def fold(index):
        return jnp.where(index <= G // 2, index, index - G).astype(F32)

    step = 2.0 * math.pi / BOX
    fy = fold(6 * position + jnp.arange(6, dtype=jnp.int32))[:, None, None]
    fx = fold(jnp.arange(G, dtype=jnp.int32))[None, :, None]
    fz = fold(jnp.arange(4 * G, dtype=jnp.int32) % G)[None, None, :]
    wave = (step * step) * (fx * fx + fy * fy + fz * fz)
    safe = jnp.where(wave > 0, wave, 1.0)
    screen = -jnp.expm1(-wave / (4.0 * OMEGA * OMEGA)) / safe
    screen = jnp.where(wave > 0, screen, 1.0 / (4.0 * OMEGA * OMEGA))
    return screen * (-2.0 * MIXING / (G * G * G))


RIGHT = [(h * 8 + z, h * 8 + (z + 1) % 8) for h in range(2) for z in range(8)]
LEFT = [(d, s) for s, d in RIGHT]
SWAP = [(i, i ^ 8) for i in range(16)]


def scatter_sources(pay, z_other, band):
    def branch(z):
        def run(own, *parts):
            moved = [own]
            for m in range(1, 8):
                pairs = [(z, (z + m) % 8), (z + 8, 8 + (z + m) % 8)]
                if z != 7:
                    pairs.append((15, 8 + (7 + m) % 8))
                moved.append(lax.ppermute(parts[m - 1], "band", pairs))
            z_here = band % 8
            pick = lambda root: lax.dynamic_index_in_dim(
                jnp.stack(moved), (z_here - root) % 8, 0, False
            )
            return pick(7), pick(z)

        return run

    parts = [
        lax.dynamic_index_in_dim(pay, (band + m) % 8, 0, False) for m in range(8)
    ]
    return lax.switch(z_other, [branch(z) for z in range(8)], *parts)


def gather_sources(pieces, mine):
    hop = lambda v, pairs: lax.ppermute(v, "band", pairs)
    other = hop(pieces, SWAP)
    both = jnp.where(mine[:, None, None, None], pieces, other)

    def step(i, carry):
        right, left, big = carry
        big = lax.dynamic_update_index_in_dim(big, left, i, 0)
        big = lax.dynamic_update_index_in_dim(big, right, (8 - i) % 8, 0)
        return hop(right, RIGHT), hop(left, LEFT), big

    big = jnp.zeros((8,) + both.shape, F32)
    _, left, big = lax.fori_loop(0, 4, step, (both, both, big))
    return lax.dynamic_update_index_in_dim(big, left, 4, 0)


def per_device(orbitals, local_potential, plan, occupancy):
    group = jnp.arange(GROUPS, dtype=jnp.int32)
    lookup = lambda g: jnp.sum(jnp.where(group == g, occupancy, 0))
    band = lax.axis_index("band")
    where = jnp.stack([band % 8, band // 8]).astype(jnp.int32)
    (mat_fy, mat_fx, mat_ix, mat_iy), (hi, lo) = jax.tree.map(jnp.asarray, tables())
    wf, wi = run_prepare(hi, lo)
    tiled = orbitals.reshape(2, OB, XP, 72, 128).transpose(0, 2, 3, 1, 4).reshape(-1, 128)
    table = screened_table(lax.axis_index("grid"))
    sec, image, potim, pay = run_section(tiled, local_potential)
    last = GROUPS - 1
    spare = jnp.where(plan[0] == last, plan[1], plan[0])
    piece_last, piece_spare = scatter_sources(pay, spare % 8, band)
    first, second = lookup(plan[0]), lookup(plan[1])
    third = jnp.where(first > 1, plan[0], plan[1])
    slots = [(plan[0], 0), (plan[1], 0), (third, 1), (plan[1], 1)]
    chosen = jnp.stack(
        [
            jnp.where(g == last, piece_last[112 * j : 112 * j + 112], piece_spare[112 * j : 112 * j + 112])
            for g, j in slots
        ]
    ).reshape(4, 2, 56, 128)
    mine = jnp.stack([g // 8 == band // 8 for g, _ in slots])

    def branch(count):
        def run(sec, image, potim, chosen, mine, table, wf, wi):
            pieces = chosen[:count]
            big = gather_sources(pieces, mine[:count])
            send = run_forward(count, where, big, sec, mat_fy, wf)
            got = lax.all_to_all(send, "grid", 0, 0, tiled=True)
            back = run_middle(count, got, table, mat_ix, mat_fx)
            got = lax.all_to_all(back, "grid", 0, 0, tiled=True)
            return tuple(run_inverse(count, where, got, big, image, sec, potim, mat_iy, wi))

        return run

    delta, sums = lax.switch(
        first + second - 2,
        [branch(2), branch(3), branch(4)],
        sec,
        image,
        potim,
        chosen,
        mine,
        table,
        wf,
        wi,
    )
    spread = jnp.broadcast_to(sums[None], (GRID, 8, 128))
    gathered = lax.all_to_all(spread, "grid", 0, 0, tiled=True)
    own_filled = lookup(band)
    filling = jnp.where(jnp.arange(OB, dtype=jnp.int32) < own_filled, 2.0, 0.0).astype(F32)
    fresh, energies = run_final(filling, gathered, tiled, run_stored(delta))
    fresh = fresh.reshape(2, XP, 72, OB, 128)
    fresh = fresh.transpose(0, 3, 1, 2, 4).reshape(orbitals.shape)
    return (fresh, energies)


def solution(mesh):
    return jax.shard_map(
        per_device,
        mesh=mesh,
        in_specs=(P(None, "band", "grid", None), P("grid", None), P(), P()),
        out_specs=(P(None, "band", "grid", None), P("band")),
        check_vma=False,
    )
```

```python
import functools
import math

import jax
import jax.numpy as jnp
import numpy as np
from jax import lax
from jax.experimental import pallas as pl
from jax.experimental.pallas import tpu as pltpu
from jax.sharding import PartitionSpec as P

G = 96
XP = 6
OB = 2
GROUPS = 16
GRID = 16
LANES = G * G
TIME_STEP = 0.4
MIXING = 0.25
OMEGA = 0.106
BOX = 65.1
BF = jnp.bfloat16
F32 = jnp.float32


def tables():
    index = np.arange(G)
    angle = (index[:, None] * index[None, :] % G) * (2.0 * math.pi / G)
    cas = np.cos(angle) + np.sin(angle)
    perm = np.array([6 * (i % 16) + i // 16 for i in range(G)])

    def halves(m):
        hi = np.asarray(m, np.float32).astype(jnp.bfloat16)
        lo = (m - hi.astype(np.float64)).astype(np.float32).astype(jnp.bfloat16)
        return hi, lo

    def extend(m):
        hi, lo = halves(m)
        return np.block([[hi, hi], [lo, np.zeros_like(lo)]])

    rows = np.array([4 * (i % 24) + i // 24 for i in range(G)])
    pads = [np.pad(h.astype(np.float32), (0, 128 - G)) for h in halves(cas)]
    mats = [cas[perm][:, rows], cas[:, perm], cas[perm], cas[rows][:, perm]]
    return [extend(m) for m in mats], pads


def split(v):
    hi = v.astype(BF)
    return hi, (v - hi.astype(F32)).astype(BF)


def dot(a, b):
    return jnp.dot(a, b, preferred_element_type=F32)


def left(mat, v):
    hi, lo = split(v)
    p = dot(mat, jnp.concatenate([hi, lo], axis=0))
    return p[:G] + p[G:]


def rows_per_dest(count):
    return -(-3 * 36 * count // 8) * 8


def prepare_kernel(hi, lo, wf, wi):
    zero = jnp.zeros((128, 128), BF)
    for f in range(4):
        for axis, out in ((1, wf), (0, wi)):
            shift = 96 * f % 128
            h = (pltpu.roll(hi[...], shift, axis) if shift else hi[...]).astype(BF)
            l = (pltpu.roll(lo[...], shift, axis) if shift else lo[...]).astype(BF)
            out[f, 0:128, 0:128] = h
            out[f, 128:256, 0:128] = h
            out[f, 0:128, 128:256] = l
            out[f, 128:256, 128:256] = zero


def section_kernel(band, plan, occupancy, psi, pot, sec, image, potim, pay, meta):
    z, ring = band[0] & 7, band[0] >> 3
    flag = lambda c: jnp.where(c, 1, 0).astype(jnp.int32)
    first, second = plan[0], plan[1]
    full = flag(occupancy[first] > 1)
    last = GROUPS - 1
    meta[0] = jnp.where(first == last, second, first) & 7
    meta[1] = full + flag(occupancy[second] > 1)
    third = jnp.where(full > 0, first, second)
    for i, g in enumerate((first, second, third, second)):
        meta[2 + i] = flag(g == last)
        meta[6 + i] = flag((g >> 3) == ring)
    for n in range(OB):
        meta[10 + n] = flag(n < occupancy[band[0]])
    meta[12] = z
    meta[13] = ring
    meta[14] = 0
    meta[15] = 0
    for t in range(72):
        a, b = t // 3, t % 3
        potim[pl.ds(24 * b + a, XP, stride=72), :] = pot[:, 128 * t : 128 * t + 128]

    @pl.loop(0, XP)
    def _(x):
        for b in range(3):
            rows = pl.ds(pl.multiple_of(72 * x + 24 * b, 8), 24)
            v = TIME_STEP * potim[rows, :]
            for n in range(OB):
                re, im = [
                    psi[pl.ds((c * XP + x) * 144 + 2 * b + n, 24, stride=6), :] for c in range(2)
                ]
                sec[0, n, rows, :] = re + v * im
                sec[1, n, rows, :] = im - v * re
                image[0, n, rows, :] = re
                image[1, n, rows, :] = im

    for c in range(2):
        for n in range(OB):
            for q in range(8):
                r = 56 * (2 * n + c)
                pay[(q + 8 - z) & 7, r : r + 54, :] = sec[c, n, 54 * q : 54 * q + 54, :]


def assemble(where, big, s, phi):
    for c in range(2):
        for q in range(8):
            rel = (q + 8 - where[0]) & 7
            phi[c, 54 * q : 54 * q + 54, :] = big[rel, s, c, 0:54, :]


def forward_kernel(count, where, big, sec, mat, wf, out, phi, yw, held):
    rt = rows_per_dest(count)
    lane = lax.broadcasted_iota(jnp.int32, (24, 128), 1)
    lane16 = lax.broadcasted_iota(jnp.int32, (16, 128), 1)

    @pl.loop(0, count)
    def _(s):
        assemble(where, big, s, phi)
        for x in range(XP):
            rows = [pl.ds(72 * x + 24 * b, 24) for b in range(3)]
            pr = [phi[0, r, :] for r in rows]
            pi = [phi[1, r, :] for r in rows]
            columns = []
            for n in range(OB):
                sr = [sec[0, n, r, :] for r in rows]
                si = [sec[1, n, r, :] for r in rows]
                for part in (
                    [pr[b] * sr[b] + pi[b] * si[b] for b in range(3)],
                    [pr[b] * si[b] - pi[b] * sr[b] for b in range(3)],
                ):
                    a, b, c = part
                    columns.append(
                        jnp.concatenate(
                            [
                                a,
                                pltpu.roll(jnp.where(lane < 96, b, a), 32, 1),
                                pltpu.roll(jnp.where(lane < 64, c, b), 64, 1),
                                pltpu.roll(c, 96, 1),
                            ],
                            axis=0,
                        )
                    )
            hi, lo = split(left(mat[...], jnp.concatenate(columns, axis=1)))
            for f in range(4):
                yw[f, pl.ds(G * x, G), 0:128] = hi[:, 128 * f : 128 * f + 128]
                yw[f, pl.ds(G * x, G), 128:256] = lo[:, 128 * f : 128 * f + 128]
        for f in range(4):
            p = dot(yw[f], wf[f])
            p = p[:, 0:128] + p[:, 128:256]
            if f:
                edge = 128 - 32 * f
                for x in range(XP):
                    for k in range(6):
                        r = G * x + 16 * k
                        start = 36 * count * (f - 1) + 36 * s + 6 * x + k
                        out[pl.ds(start, 16, stride=rt), :] = jnp.where(
                            lane16 < edge, held[pl.ds(r, 16), :], p[r : r + 16]
                        )
            if f < 3:
                held[...] = p


def middle_kernel(count, rec, table, mat1, mat2, out):
    rt = rows_per_dest(count)

    @pl.loop(0, count)
    def _(s):
        for kk in range(3):
            starts = [
                [36 * count * t + 36 * s + 6 * x + k for x in range(XP)]
                for k in (2 * kk, 2 * kk + 1)
                for t in range(3)
            ]
            v = jnp.concatenate(
                [
                    jnp.concatenate([rec[pl.ds(r, 16, stride=rt), :] for r in st], axis=0)
                    for st in starts
                ],
                axis=1,
            )
            v = left(mat2[...], v) * jnp.concatenate([table[2 * kk], table[2 * kk + 1]], axis=1)
            v = left(mat1[...], v)
            for i, st in enumerate(starts):
                for x in range(XP):
                    out[pl.ds(st[x], 16, stride=rt), :] = v[
                        16 * x : 16 * x + 16, 128 * i : 128 * i + 128
                    ]


def inverse_kernel(
    count, where, rec, big, image, sec, potim, mat, wi, delta, sums, phi, xw, wide, acc
):
    rt = rows_per_dest(count)
    lane = lax.broadcasted_iota(jnp.int32, (24, 128), 1)
    laneg = lax.broadcasted_iota(jnp.int32, (G, 128), 1)
    acc[...] = jnp.zeros_like(acc)

    @pl.loop(0, count)
    def _(s):
        assemble(where, big, s, phi)
        for x in range(XP):
            a, b, c = [
                jnp.concatenate(
                    [
                        rec[pl.ds(36 * count * t + 36 * s + 6 * x + k, 16, stride=rt), :]
                        for k in range(6)
                    ],
                    axis=0,
                )
                for t in range(3)
            ]
            fields = [a, jnp.where(laneg < 64, b, a), jnp.where(laneg < 32, c, b), c]
            for f in range(4):
                hi, lo = split(fields[f])
                xw[f, pl.ds(G * x, G), 0:128] = hi
                xw[f, pl.ds(G * x, G), 128:256] = lo
        for f in range(4):
            p = dot(xw[f], wi[f])
            wide[f] = p[:, 0:128] + p[:, 128:256]
        for x in range(XP):
            v = jnp.concatenate([wide[f, pl.ds(G * x, G), :] for f in range(4)], axis=1)
            v = left(mat[...], v)
            rows = [pl.ds(72 * x + 24 * b, 24) for b in range(3)]
            for n in range(OB):
                field = []
                for ri in range(2):
                    f = 2 * n + ri
                    y = [v[24 * i : 24 * i + 24, 128 * f : 128 * f + 128] for i in range(4)]
                    r1 = pltpu.roll(y[1], 96, 1)
                    r2 = pltpu.roll(y[2], 64, 1)
                    r3 = pltpu.roll(y[3], 32, 1)
                    field.append(
                        [
                            jnp.where(lane < 96, y[0], r1),
                            jnp.where(lane < 64, r1, r2),
                            jnp.where(lane < 32, r2, r3),
                        ]
                    )
                for b in range(3):
                    pr, pi = phi[0, rows[b], :], phi[1, rows[b], :]
                    vr, vi = field[0][b], field[1][b]
                    acc[0, n, rows[b], :] += pr * vr - pi * vi
                    acc[1, n, rows[b], :] += pr * vi + pi * vr

    def tail(i, carry):
        carry = list(carry)
        rows = pl.ds(pl.multiple_of(24 * i, 8), 24)
        v = potim[rows, :]
        for n in range(OB):
            re, im = image[0, n, rows, :], image[1, n, rows, :]
            sr, si = sec[0, n, rows, :], sec[1, n, rows, :]
            hr = v * sr + acc[0, n, rows, :]
            hi = v * si + acc[1, n, rows, :]
            dr = (0.5 * TIME_STEP) * (v * im + hi)
            di = (0.5 * TIME_STEP) * (-v * re - hr)
            delta[0, n, rows, :] = dr
            delta[1, n, rows, :] = di
            carry[n] = carry[n] + (re * dr + im * di)
            carry[2 + n] = carry[2 + n] + (dr * dr + di * di)
            carry[4 + n] = carry[4 + n] + (sr * hr + si * hi)
        return tuple(carry)

    zero = jnp.zeros((24, 128), F32)
    carry = lax.fori_loop(0, 18, tail, (zero,) * 6)
    rows = [jnp.sum(c, axis=0, keepdims=True) for c in carry]
    sums[...] = jnp.concatenate(rows + [jnp.zeros((2, 128), F32)], axis=0)


def stored_kernel(delta, out):
    @pl.loop(0, XP)
    def _(x):
        for c in range(2):
            for n in range(OB):
                for b in range(3):
                    rows = pl.ds(pl.multiple_of(72 * x + 24 * b, 8), 24)
                    out[pl.ds((c * XP + x) * 144 + 2 * b + n, 24, stride=6), :] = delta[
                        c, n, rows, :
                    ]


def final_kernel(filling, gathered, psi, delta, out, energies):
    t = jnp.sum(jnp.sum(gathered[...], axis=0), axis=1, keepdims=True)
    factor = -2.0 * t[0:2] / (t[2:4] + 1e-06)
    odd = lax.broadcasted_iota(jnp.int32, (216, 128), 0) % OB == 1
    scale = jnp.where(odd, factor[1:2], factor[0:1])

    @pl.loop(0, 8)
    def _(i):
        rows = pl.ds(pl.multiple_of(216 * i, 8), 216)
        out[rows, :] = psi[rows, :] + scale * delta[rows, :]

    for n in range(OB):
        energies[n] = filling[n] * t[4 + n, 0] / (G * G * G)


VM = pl.BlockSpec(memory_space=pltpu.VMEM)
SM = pl.BlockSpec(memory_space=pltpu.SMEM)


def shape(*dims):
    return jax.ShapeDtypeStruct(dims, F32)


def call(kernel, outs, ins, scratch=(), smem=0, flops=0, moved=0):
    return pl.pallas_call(
        kernel,
        out_shape=outs,
        in_specs=[SM] * smem + [VM] * (len(ins) - smem),
        out_specs=[VM] * len(outs),
        scratch_shapes=list(scratch),
        cost_estimate=pl.CostEstimate(flops=flops, bytes_accessed=moved, transcendentals=0),
    )(*ins)


def run_prepare(hi, lo):
    wide = jax.ShapeDtypeStruct((4, 256, 256), BF)
    return call(prepare_kernel, [wide, wide], [hi, lo], moved=2 << 20)


def run_section(band, plan, occupancy, psi, pot):
    return pl.pallas_call(
        section_kernel,
        out_shape=[
            shape(2, OB, 432, 128),
            shape(2, OB, 432, 128),
            shape(432, 128),
            shape(8, 224, 128),
            jax.ShapeDtypeStruct((16,), jnp.int32),
        ],
        in_specs=[SM, SM, SM, VM, VM],
        out_specs=[VM, VM, VM, VM, SM],
        cost_estimate=pl.CostEstimate(flops=1 << 20, bytes_accessed=4 << 20, transcendentals=0),
    )(band, plan, occupancy, psi, pot)


def run_stored(delta):
    return call(stored_kernel, [shape(1728, 128)], [delta], moved=2 << 20)[0]


def run_final(filling, gathered, psi, delta):
    return pl.pallas_call(
        final_kernel,
        out_shape=[shape(1728, 128), shape(OB)],
        in_specs=[SM, VM, VM, VM],
        out_specs=[VM, SM],
        cost_estimate=pl.CostEstimate(flops=1 << 20, bytes_accessed=3 << 20, transcendentals=0),
    )(filling, gathered, psi, delta)


def run_forward(count, where, big, sec, mat, wf):
    rows = GRID * rows_per_dest(count)
    return call(
        functools.partial(forward_kernel, count),
        [shape(rows, 128)],
        [where, big, sec, mat, wf],
        [
            pltpu.VMEM((2, 432, 128), F32),
            pltpu.VMEM((4, XP * G, 256), BF),
            pltpu.VMEM((XP * G, 128), F32),
        ],
        smem=1,
        flops=count << 30,
        moved=count << 21,
    )[0]


def run_middle(count, rec, table, mat1, mat2):
    rows = GRID * rows_per_dest(count)
    return call(
        functools.partial(middle_kernel, count),
        [shape(rows, 128)],
        [rec, table, mat1, mat2],
        flops=count << 30,
        moved=count << 21,
    )[0]


def run_inverse(count, where, rec, big, image, sec, potim, mat, wi):
    return call(
        functools.partial(inverse_kernel, count),
        [shape(2, OB, 432, 128), shape(8, 128)],
        [where, rec, big, image, sec, potim, mat, wi],
        [
            pltpu.VMEM((2, 432, 128), F32),
            pltpu.VMEM((4, XP * G, 256), BF),
            pltpu.VMEM((4, XP * G, 128), F32),
            pltpu.VMEM((2, OB, 432, 128), F32),
        ],
        smem=1,
        flops=count << 30,
        moved=count << 21,
    )


def screened_table(position):
    def fold(index):
        return jnp.where(index <= G // 2, index, index - G).astype(F32)

    step = 2.0 * math.pi / BOX
    fy = fold(6 * position + jnp.arange(6, dtype=jnp.int32))[:, None, None]
    fx = fold(jnp.arange(G, dtype=jnp.int32))[None, :, None]
    fz = fold(jnp.arange(4 * G, dtype=jnp.int32) % G)[None, None, :]
    wave = (step * step) * (fx * fx + fy * fy + fz * fz)
    safe = jnp.where(wave > 0, wave, 1.0)
    screen = -jnp.expm1(-wave / (4.0 * OMEGA * OMEGA)) / safe
    screen = jnp.where(wave > 0, screen, 1.0 / (4.0 * OMEGA * OMEGA))
    return screen * (-2.0 * MIXING / (G * G * G))


RIGHT = [(h * 8 + z, h * 8 + (z + 1) % 8) for h in range(2) for z in range(8)]
LEFT = [(d, s) for s, d in RIGHT]
SWAP = [(i, i ^ 8) for i in range(16)]


def scatter_sources(pay, z_other, z_here):
    def branch(z):
        def run(pay, z_here):
            moved = [pay[0]]
            for m in range(1, 8):
                pairs = [(z, (z + m) % 8), (z + 8, 8 + (z + m) % 8)]
                if z != 7:
                    pairs.append((15, 8 + (7 + m) % 8))
                moved.append(lax.ppermute(pay[m], "band", pairs))
            moved = jnp.stack(moved)

            def pick(root):
                return lax.dynamic_index_in_dim(moved, (z_here + (8 - root)) & 7, 0, False)

            return pick(7), pick(z)

        return run

    return lax.switch(z_other, [branch(z) for z in range(8)], pay, z_here)


def gather_sources(both):
    hop = lambda v, pairs: lax.ppermute(v, "band", pairs)

    def step(i, carry):
        right, left, big = carry
        big = lax.dynamic_update_index_in_dim(big, left, i, 0)
        big = lax.dynamic_update_index_in_dim(big, right, (8 - i) % 8, 0)
        return hop(right, RIGHT), hop(left, LEFT), big

    big = jnp.zeros((8,) + both.shape, F32)
    _, left, big = lax.fori_loop(0, 4, step, (both, both, big))
    return lax.dynamic_update_index_in_dim(big, left, 4, 0)


def per_device(orbitals, local_potential, plan, occupancy):
    band = lax.axis_index("band").astype(jnp.int32).reshape(1)
    mats, (hi, lo) = jax.tree.map(jnp.asarray, tables())
    mat_fy, mat_fx, mat_ix, mat_iy = mats
    tiled = orbitals.reshape(2, OB, XP, 72, 128).transpose(0, 2, 3, 1, 4).reshape(-1, 128)
    sec, image, potim, pay, meta = run_section(band, plan, occupancy, tiled, local_potential)
    where = meta[12:14]
    piece_last, piece_spare = scatter_sources(pay, meta[0], meta[12])
    flags = lambda k: (meta[k : k + 4] > 0)[:, None, None, None]
    rows = [slice(112 * j, 112 * j + 112) for j in (0, 0, 1, 1)]
    chosen = jnp.where(
        flags(2),
        jnp.stack([piece_last[r] for r in rows]).reshape(4, 2, 56, 128),
        jnp.stack([piece_spare[r] for r in rows]).reshape(4, 2, 56, 128),
    )
    position = lax.axis_index("grid")
    chosen, position, hi, lo = lax.optimization_barrier((chosen, position, hi, lo))
    other = lax.ppermute(chosen, "band", SWAP)
    wf, wi = run_prepare(hi, lo)
    table = screened_table(position)
    both = jnp.where(flags(6), chosen, other)

    def branch(count):
        def run(sec, image, potim, both, table, wf, wi, where):
            big = gather_sources(both[:count])
            send = run_forward(count, where, big, sec, mat_fy, wf)
            got = lax.all_to_all(send, "grid", 0, 0, tiled=True)
            back = run_middle(count, got, table, mat_ix, mat_fx)
            got = lax.all_to_all(back, "grid", 0, 0, tiled=True)
            return tuple(run_inverse(count, where, got, big, image, sec, potim, mat_iy, wi))

        return run

    delta, sums = lax.switch(
        meta[1],
        [branch(2), branch(3), branch(4)],
        sec,
        image,
        potim,
        both,
        table,
        wf,
        wi,
        where,
    )
    spread = jnp.broadcast_to(sums[None], (GRID, 8, 128))
    gathered = lax.all_to_all(spread, "grid", 0, 0, tiled=True)
    filling = 2.0 * meta[10:12].astype(F32)
    fresh, energies = run_final(filling, gathered, tiled, run_stored(delta))
    fresh = fresh.reshape(2, XP, 72, OB, 128)
    fresh = fresh.transpose(0, 3, 1, 2, 4).reshape(orbitals.shape)
    return (fresh, energies)


def solution(mesh):
    return jax.shard_map(
        per_device,
        mesh=mesh,
        in_specs=(P(None, "band", "grid", None), P("grid", None), P(), P()),
        out_specs=(P(None, "band", "grid", None), P("band")),
        check_vma=False,
    )
```

```python
import functools
import math

import jax
import jax.numpy as jnp
import numpy as np
from jax import lax
from jax.experimental import pallas as pl
from jax.experimental.pallas import tpu as pltpu
from jax.sharding import PartitionSpec as P

G = 96
XP = 6
OB = 2
GROUPS = 16
GRID = 16
LANES = G * G
TIME_STEP = 0.4
MIXING = 0.25
OMEGA = 0.106
BOX = 65.1
BF = jnp.bfloat16
F32 = jnp.float32


def tables():
    index = np.arange(G)
    angle = (index[:, None] * index[None, :] % G) * (2.0 * math.pi / G)
    cas = np.cos(angle) + np.sin(angle)
    perm = np.array([6 * (i % 16) + i // 16 for i in range(G)])

    def halves(m):
        hi = np.asarray(m, np.float32).astype(jnp.bfloat16)
        lo = (m - hi.astype(np.float64)).astype(np.float32).astype(jnp.bfloat16)
        return hi, lo

    def extend(m):
        hi, lo = halves(m)
        return np.block([[hi, hi], [lo, np.zeros_like(lo)]])

    rows = np.array([4 * (i % 24) + i // 24 for i in range(G)])
    pads = [np.pad(h.astype(np.float32), (0, 128 - G)) for h in halves(cas)]
    mats = [cas[perm][:, rows], cas[:, perm], cas[perm], cas[rows][:, perm]]
    return [extend(m) for m in mats], pads


def split(v):
    hi = v.astype(BF)
    return hi, (v - hi.astype(F32)).astype(BF)


def dot(a, b):
    return jnp.dot(a, b, preferred_element_type=F32)


def left(mat, v):
    hi, lo = split(v)
    p = dot(mat, jnp.concatenate([hi, lo], axis=0))
    return p[:G] + p[G:]


def rows_per_dest(count):
    return -(-3 * 36 * count // 8) * 8


def prepare_kernel(hi, lo, wf, wi):
    zero = jnp.zeros((128, 128), BF)
    for f in range(4):
        for axis, out in ((1, wf), (0, wi)):
            shift = 96 * f % 128
            h = (pltpu.roll(hi[...], shift, axis) if shift else hi[...]).astype(BF)
            l = (pltpu.roll(lo[...], shift, axis) if shift else lo[...]).astype(BF)
            out[f, 0:128, 0:128] = h
            out[f, 128:256, 0:128] = h
            out[f, 0:128, 128:256] = l
            out[f, 128:256, 128:256] = zero


def section_kernel(band, plan, occupancy, psi, pot, sec, image, potim, pay, meta):
    z, ring = band[0] & 7, band[0] >> 3
    flag = lambda c: jnp.where(c, 1, 0).astype(jnp.int32)
    first, second = plan[0], plan[1]
    full = flag(occupancy[first] > 1)
    last = GROUPS - 1
    meta[0] = jnp.where(first == last, second, first) & 7
    meta[1] = full + flag(occupancy[second] > 1)
    third = jnp.where(full > 0, first, second)
    for i, g in enumerate((first, second, third, second)):
        meta[2 + i] = flag(g == last)
        meta[6 + i] = flag((g >> 3) == ring)
    for n in range(OB):
        meta[10 + n] = flag(n < occupancy[band[0]])
    meta[12] = z
    meta[13] = ring
    meta[14] = 0
    meta[15] = 0
    for t in range(72):
        a, b = t // 3, t % 3
        potim[pl.ds(24 * b + a, XP, stride=72), :] = pot[:, 128 * t : 128 * t + 128]

    @pl.loop(0, XP)
    def _(x):
        for b in range(3):
            rows = pl.ds(pl.multiple_of(72 * x + 24 * b, 8), 24)
            v = TIME_STEP * potim[rows, :]
            for n in range(OB):
                re, im = [
                    psi[pl.ds((c * XP + x) * 144 + 2 * b + n, 24, stride=6), :] for c in range(2)
                ]
                sec[0, n, rows, :] = re + v * im
                sec[1, n, rows, :] = im - v * re
                image[0, n, rows, :] = re
                image[1, n, rows, :] = im

    for c in range(2):
        for n in range(OB):
            for q in range(8):
                r = 56 * (2 * n + c)
                pay[(q + 8 - z) & 7, r : r + 54, :] = sec[c, n, 54 * q : 54 * q + 54, :]


def pick_kernel(meta, *refs):
    out = refs[8]
    for kind, root in ((1, 7), (0, meta[0])):
        distance = (meta[12] + 8 - root) & 7
        for m in range(8):

            @pl.when(distance == m)
            def _():
                for i, j in enumerate((0, 0, 1, 1)):

                    @pl.when(meta[2 + i] == kind)
                    def _():
                        out[i] = refs[m][112 * j : 112 * j + 112, :]


def assemble(where, big, s, phi):
    for c in range(2):
        for q in range(8):
            rel = (q + 8 - where[0]) & 7
            phi[c, 54 * q : 54 * q + 54, :] = big[rel, s, c, 0:54, :]


def forward_kernel(count, where, big, sec, mat, wf, out, phi, yw, held):
    rt = rows_per_dest(count)
    lane = lax.broadcasted_iota(jnp.int32, (24, 128), 1)
    lane16 = lax.broadcasted_iota(jnp.int32, (16, 128), 1)

    @pl.loop(0, count)
    def _(s):
        assemble(where, big, s, phi)
        for x in range(XP):
            rows = [pl.ds(72 * x + 24 * b, 24) for b in range(3)]
            pr = [phi[0, r, :] for r in rows]
            pi = [phi[1, r, :] for r in rows]
            columns = []
            for n in range(OB):
                sr = [sec[0, n, r, :] for r in rows]
                si = [sec[1, n, r, :] for r in rows]
                for part in (
                    [pr[b] * sr[b] + pi[b] * si[b] for b in range(3)],
                    [pr[b] * si[b] - pi[b] * sr[b] for b in range(3)],
                ):
                    a, b, c = part
                    columns.append(
                        jnp.concatenate(
                            [
                                a,
                                pltpu.roll(jnp.where(lane < 96, b, a), 32, 1),
                                pltpu.roll(jnp.where(lane < 64, c, b), 64, 1),
                                pltpu.roll(c, 96, 1),
                            ],
                            axis=0,
                        )
                    )
            hi, lo = split(left(mat[...], jnp.concatenate(columns, axis=1)))
            for f in range(4):
                yw[f, pl.ds(G * x, G), 0:128] = hi[:, 128 * f : 128 * f + 128]
                yw[f, pl.ds(G * x, G), 128:256] = lo[:, 128 * f : 128 * f + 128]
        for f in range(4):
            p = dot(yw[f], wf[f])
            p = p[:, 0:128] + p[:, 128:256]
            if f:
                edge = 128 - 32 * f
                for x in range(XP):
                    for k in range(6):
                        r = G * x + 16 * k
                        start = 36 * count * (f - 1) + 36 * s + 6 * x + k
                        out[pl.ds(start, 16, stride=rt), :] = jnp.where(
                            lane16 < edge, held[pl.ds(r, 16), :], p[r : r + 16]
                        )
            if f < 3:
                held[...] = p


def middle_kernel(count, rec, table, mat1, mat2, out):
    rt = rows_per_dest(count)

    @pl.loop(0, count)
    def _(s):
        for kk in range(3):
            starts = [
                [36 * count * t + 36 * s + 6 * x + k for x in range(XP)]
                for k in (2 * kk, 2 * kk + 1)
                for t in range(3)
            ]
            v = jnp.concatenate(
                [
                    jnp.concatenate([rec[pl.ds(r, 16, stride=rt), :] for r in st], axis=0)
                    for st in starts
                ],
                axis=1,
            )
            v = left(mat2[...], v) * jnp.concatenate([table[2 * kk], table[2 * kk + 1]], axis=1)
            v = left(mat1[...], v)
            for i, st in enumerate(starts):
                for x in range(XP):
                    out[pl.ds(st[x], 16, stride=rt), :] = v[
                        16 * x : 16 * x + 16, 128 * i : 128 * i + 128
                    ]


def inverse_kernel(
    count, where, rec, big, image, sec, potim, mat, wi, delta, sums, phi, xw, wide, acc
):
    rt = rows_per_dest(count)
    lane = lax.broadcasted_iota(jnp.int32, (24, 128), 1)
    laneg = lax.broadcasted_iota(jnp.int32, (G, 128), 1)
    acc[...] = jnp.zeros_like(acc)

    @pl.loop(0, count)
    def _(s):
        assemble(where, big, s, phi)
        for x in range(XP):
            a, b, c = [
                jnp.concatenate(
                    [
                        rec[pl.ds(36 * count * t + 36 * s + 6 * x + k, 16, stride=rt), :]
                        for k in range(6)
                    ],
                    axis=0,
                )
                for t in range(3)
            ]
            fields = [a, jnp.where(laneg < 64, b, a), jnp.where(laneg < 32, c, b), c]
            for f in range(4):
                hi, lo = split(fields[f])
                xw[f, pl.ds(G * x, G), 0:128] = hi
                xw[f, pl.ds(G * x, G), 128:256] = lo
        for f in range(4):
            p = dot(xw[f], wi[f])
            wide[f] = p[:, 0:128] + p[:, 128:256]
        for x in range(XP):
            v = jnp.concatenate([wide[f, pl.ds(G * x, G), :] for f in range(4)], axis=1)
            v = left(mat[...], v)
            rows = [pl.ds(72 * x + 24 * b, 24) for b in range(3)]
            for n in range(OB):
                field = []
                for ri in range(2):
                    f = 2 * n + ri
                    y = [v[24 * i : 24 * i + 24, 128 * f : 128 * f + 128] for i in range(4)]
                    r1 = pltpu.roll(y[1], 96, 1)
                    r2 = pltpu.roll(y[2], 64, 1)
                    r3 = pltpu.roll(y[3], 32, 1)
                    field.append(
                        [
                            jnp.where(lane < 96, y[0], r1),
                            jnp.where(lane < 64, r1, r2),
                            jnp.where(lane < 32, r2, r3),
                        ]
                    )
                for b in range(3):
                    pr, pi = phi[0, rows[b], :], phi[1, rows[b], :]
                    vr, vi = field[0][b], field[1][b]
                    acc[0, n, rows[b], :] += pr * vr - pi * vi
                    acc[1, n, rows[b], :] += pr * vi + pi * vr

    def tail(i, carry):
        carry = list(carry)
        rows = pl.ds(pl.multiple_of(24 * i, 8), 24)
        v = potim[rows, :]
        for n in range(OB):
            re, im = image[0, n, rows, :], image[1, n, rows, :]
            sr, si = sec[0, n, rows, :], sec[1, n, rows, :]
            hr = v * sr + acc[0, n, rows, :]
            hi = v * si + acc[1, n, rows, :]
            dr = (0.5 * TIME_STEP) * (v * im + hi)
            di = (0.5 * TIME_STEP) * (-v * re - hr)
            delta[0, n, rows, :] = dr
            delta[1, n, rows, :] = di
            carry[n] = carry[n] + (re * dr + im * di)
            carry[2 + n] = carry[2 + n] + (dr * dr + di * di)
            carry[4 + n] = carry[4 + n] + (sr * hr + si * hi)
        return tuple(carry)

    zero = jnp.zeros((24, 128), F32)
    carry = lax.fori_loop(0, 18, tail, (zero,) * 6)
    rows = [jnp.sum(c, axis=0, keepdims=True) for c in carry]
    sums[...] = jnp.concatenate(rows + [jnp.zeros((2, 128), F32)], axis=0)


def stored_kernel(delta, out):
    @pl.loop(0, XP)
    def _(x):
        for c in range(2):
            for n in range(OB):
                for b in range(3):
                    rows = pl.ds(pl.multiple_of(72 * x + 24 * b, 8), 24)
                    out[pl.ds((c * XP + x) * 144 + 2 * b + n, 24, stride=6), :] = delta[
                        c, n, rows, :
                    ]


def final_kernel(filling, gathered, psi, delta, out, energies):
    t = jnp.sum(jnp.sum(gathered[...], axis=0), axis=1, keepdims=True)
    factor = -2.0 * t[0:2] / (t[2:4] + 1e-06)
    odd = lax.broadcasted_iota(jnp.int32, (216, 128), 0) % OB == 1
    scale = jnp.where(odd, factor[1:2], factor[0:1])

    @pl.loop(0, 8)
    def _(i):
        rows = pl.ds(pl.multiple_of(216 * i, 8), 216)
        out[rows, :] = psi[rows, :] + scale * delta[rows, :]

    for n in range(OB):
        energies[n] = filling[n] * t[4 + n, 0] / (G * G * G)


VM = pl.BlockSpec(memory_space=pltpu.VMEM)
SM = pl.BlockSpec(memory_space=pltpu.SMEM)


def shape(*dims):
    return jax.ShapeDtypeStruct(dims, F32)


def call(kernel, outs, ins, scratch=(), smem=0, flops=0, moved=0):
    return pl.pallas_call(
        kernel,
        out_shape=outs,
        in_specs=[SM] * smem + [VM] * (len(ins) - smem),
        out_specs=[VM] * len(outs),
        scratch_shapes=list(scratch),
        cost_estimate=pl.CostEstimate(flops=flops, bytes_accessed=moved, transcendentals=0),
    )(*ins)


def run_prepare(hi, lo):
    wide = jax.ShapeDtypeStruct((4, 256, 256), BF)
    return call(prepare_kernel, [wide, wide], [hi, lo], moved=2 << 20)


def run_section(band, plan, occupancy, psi, pot):
    return pl.pallas_call(
        section_kernel,
        out_shape=[
            shape(2, OB, 432, 128),
            shape(2, OB, 432, 128),
            shape(432, 128),
            shape(8, 224, 128),
            jax.ShapeDtypeStruct((16,), jnp.int32),
        ],
        in_specs=[SM, SM, SM, VM, VM],
        out_specs=[VM, VM, VM, VM, SM],
        cost_estimate=pl.CostEstimate(flops=1 << 20, bytes_accessed=4 << 20, transcendentals=0),
    )(band, plan, occupancy, psi, pot)


def run_pick(meta, pieces):
    return call(pick_kernel, [shape(4, 112, 128)], [meta, *pieces], smem=1, moved=1 << 20)[0]


def run_stored(delta):
    return call(stored_kernel, [shape(1728, 128)], [delta], moved=2 << 20)[0]


def run_final(filling, gathered, psi, delta):
    return pl.pallas_call(
        final_kernel,
        out_shape=[shape(1728, 128), shape(OB)],
        in_specs=[SM, VM, VM, VM],
        out_specs=[VM, SM],
        cost_estimate=pl.CostEstimate(flops=1 << 20, bytes_accessed=3 << 20, transcendentals=0),
    )(filling, gathered, psi, delta)


def run_forward(count, where, big, sec, mat, wf):
    rows = GRID * rows_per_dest(count)
    return call(
        functools.partial(forward_kernel, count),
        [shape(rows, 128)],
        [where, big, sec, mat, wf],
        [
            pltpu.VMEM((2, 432, 128), F32),
            pltpu.VMEM((4, XP * G, 256), BF),
            pltpu.VMEM((XP * G, 128), F32),
        ],
        smem=1,
        flops=count << 30,
        moved=count << 21,
    )[0]


def run_middle(count, rec, table, mat1, mat2):
    rows = GRID * rows_per_dest(count)
    return call(
        functools.partial(middle_kernel, count),
        [shape(rows, 128)],
        [rec, table, mat1, mat2],
        flops=count << 30,
        moved=count << 21,
    )[0]


def run_inverse(count, where, rec, big, image, sec, potim, mat, wi):
    return call(
        functools.partial(inverse_kernel, count),
        [shape(2, OB, 432, 128), shape(8, 128)],
        [where, rec, big, image, sec, potim, mat, wi],
        [
            pltpu.VMEM((2, 432, 128), F32),
            pltpu.VMEM((4, XP * G, 256), BF),
            pltpu.VMEM((4, XP * G, 128), F32),
            pltpu.VMEM((2, OB, 432, 128), F32),
        ],
        smem=1,
        flops=count << 30,
        moved=count << 21,
    )


def screened_table(position):
    def fold(index):
        return jnp.where(index <= G // 2, index, index - G).astype(F32)

    step = 2.0 * math.pi / BOX
    fy = fold(6 * position + jnp.arange(6, dtype=jnp.int32))[:, None, None]
    fx = fold(jnp.arange(G, dtype=jnp.int32))[None, :, None]
    fz = fold(jnp.arange(4 * G, dtype=jnp.int32) % G)[None, None, :]
    wave = (step * step) * (fx * fx + fy * fy + fz * fz)
    safe = jnp.where(wave > 0, wave, 1.0)
    screen = -jnp.expm1(-wave / (4.0 * OMEGA * OMEGA)) / safe
    screen = jnp.where(wave > 0, screen, 1.0 / (4.0 * OMEGA * OMEGA))
    return screen * (-2.0 * MIXING / (G * G * G))


RIGHT = [(h * 8 + z, h * 8 + (z + 1) % 8) for h in range(2) for z in range(8)]
LEFT = [(d, s) for s, d in RIGHT]
SWAP = [(i, i ^ 8) for i in range(16)]


def shifted(m):
    return [(h * 8 + z, h * 8 + (z + m) % 8) for h in range(2) for z in range(8)]


def gather_sources(both):
    hop = lambda v, pairs: lax.ppermute(v, "band", pairs)

    def step(i, carry):
        right, left, big = carry
        big = lax.dynamic_update_index_in_dim(big, left, i, 0)
        big = lax.dynamic_update_index_in_dim(big, right, (8 - i) % 8, 0)
        return hop(right, RIGHT), hop(left, LEFT), big

    big = jnp.zeros((8,) + both.shape, F32)
    _, left, big = lax.fori_loop(0, 4, step, (both, both, big))
    return lax.dynamic_update_index_in_dim(big, left, 4, 0)


def per_device(orbitals, local_potential, plan, occupancy):
    band = lax.axis_index("band").astype(jnp.int32).reshape(1)
    mats, (hi, lo) = jax.tree.map(jnp.asarray, tables())
    mat_fy, mat_fx, mat_ix, mat_iy = mats
    tiled = orbitals.reshape(2, OB, XP, 72, 128).transpose(0, 2, 3, 1, 4).reshape(-1, 128)
    sec, image, potim, pay, meta = run_section(band, plan, occupancy, tiled, local_potential)
    where = meta[12:14]
    flags = lambda k: (meta[k : k + 4] > 0)[:, None, None, None]
    pay, position, hi, lo = lax.optimization_barrier((pay, lax.axis_index("grid"), hi, lo))
    pieces = [pay[0]] + [lax.ppermute(pay[m], "band", shifted(m)) for m in range(1, 8)]
    chosen = run_pick(meta, pieces).reshape(4, 2, 56, 128)
    other = lax.ppermute(chosen, "band", SWAP)
    wf, wi = run_prepare(hi, lo)
    table = screened_table(position)
    both = jnp.where(flags(6), chosen, other)

    def branch(count):
        def run(sec, image, potim, both, table, wf, wi, where):
            big = gather_sources(both[:count])
            send = run_forward(count, where, big, sec, mat_fy, wf)
            got = lax.all_to_all(send, "grid", 0, 0, tiled=True)
            back = run_middle(count, got, table, mat_ix, mat_fx)
            got = lax.all_to_all(back, "grid", 0, 0, tiled=True)
            return tuple(run_inverse(count, where, got, big, image, sec, potim, mat_iy, wi))

        return run

    delta, sums = lax.switch(
        meta[1],
        [branch(2), branch(3), branch(4)],
        sec,
        image,
        potim,
        both,
        table,
        wf,
        wi,
        where,
    )
    spread = jnp.broadcast_to(sums[None], (GRID, 8, 128))
    gathered = lax.all_to_all(spread, "grid", 0, 0, tiled=True)
    filling = 2.0 * meta[10:12].astype(F32)
    fresh, energies = run_final(filling, gathered, tiled, run_stored(delta))
    fresh = fresh.reshape(2, XP, 72, OB, 128)
    fresh = fresh.transpose(0, 3, 1, 2, 4).reshape(orbitals.shape)
    return (fresh, energies)


def solution(mesh):
    return jax.shard_map(
        per_device,
        mesh=mesh,
        in_specs=(P(None, "band", "grid", None), P("grid", None), P(), P()),
        out_specs=(P(None, "band", "grid", None), P("band")),
        check_vma=False,
    )
```

```python
import functools
import math

import jax
import jax.numpy as jnp
import numpy as np
from jax import lax
from jax.experimental import pallas as pl
from jax.experimental.pallas import tpu as pltpu
from jax.sharding import PartitionSpec as P

G = 96
XP = 6
OB = 2
GROUPS = 16
GRID = 16
LANES = G * G
TIME_STEP = 0.4
MIXING = 0.25
OMEGA = 0.106
BOX = 65.1
BF = jnp.bfloat16
F32 = jnp.float32


def tables():
    index = np.arange(G)
    angle = (index[:, None] * index[None, :] % G) * (2.0 * math.pi / G)
    cas = np.cos(angle) + np.sin(angle)
    perm = np.array([6 * (i % 16) + i // 16 for i in range(G)])

    def halves(m):
        hi = np.asarray(m, np.float32).astype(jnp.bfloat16)
        lo = (m - hi.astype(np.float64)).astype(np.float32).astype(jnp.bfloat16)
        return hi, lo

    def extend(m):
        hi, lo = halves(m)
        return np.block([[hi, hi], [lo, np.zeros_like(lo)]])

    rows = np.array([4 * (i % 24) + i // 24 for i in range(G)])
    pads = [np.pad(h.astype(np.float32), (0, 128 - G)) for h in halves(cas)]
    mats = [cas[perm][:, rows], cas[:, perm], cas[perm], cas[rows][:, perm]]
    return [extend(m) for m in mats], pads


def split(v):
    hi = v.astype(BF)
    return hi, (v - hi.astype(F32)).astype(BF)


def dot(a, b):
    return jnp.dot(a, b, preferred_element_type=F32)


def left(mat, v):
    hi, lo = split(v)
    p = dot(mat, jnp.concatenate([hi, lo], axis=0))
    return p[:G] + p[G:]


def rows_per_dest(count):
    return -(-3 * 36 * count // 8) * 8


def prepare_kernel(hi, lo, wf, wi):
    zero = jnp.zeros((128, 128), BF)
    for f in range(4):
        for axis, out in ((1, wf), (0, wi)):
            shift = 96 * f % 128
            h = (pltpu.roll(hi[...], shift, axis) if shift else hi[...]).astype(BF)
            l = (pltpu.roll(lo[...], shift, axis) if shift else lo[...]).astype(BF)
            out[f, 0:128, 0:128] = h
            out[f, 128:256, 0:128] = h
            out[f, 0:128, 128:256] = l
            out[f, 128:256, 128:256] = zero


def section_kernel(psi, pot, sec, image, potim, pay):
    for t in range(72):
        a, b = t // 3, t % 3
        potim[pl.ds(24 * b + a, XP, stride=72), :] = pot[:, 128 * t : 128 * t + 128]

    @pl.loop(0, XP)
    def _(x):
        for b in range(3):
            rows = pl.ds(pl.multiple_of(72 * x + 24 * b, 8), 24)
            v = TIME_STEP * potim[rows, :]
            for n in range(OB):
                re, im = [
                    psi[pl.ds((c * XP + x) * 144 + 2 * b + n, 24, stride=6), :] for c in range(2)
                ]
                sec[0, n, rows, :] = re + v * im
                sec[1, n, rows, :] = im - v * re
                image[0, n, rows, :] = re
                image[1, n, rows, :] = im

    for c in range(2):
        for n in range(OB):
            for q in range(8):
                pay[8 * c + q, 56 * n : 56 * n + 54, :] = sec[c, n, 54 * q : 54 * q + 54, :]


def assemble(where, big, s, phi):
    for c in range(2):
        for q in range(8):
            rel = (q + 8 - where[0]) & 7
            phi[c, 54 * q : 54 * q + 54, :] = big[rel, c ^ where[1], s, 0:54, :]


def forward_kernel(count, where, big, sec, mat, wf, out, phi, yw, held):
    rt = rows_per_dest(count)
    lane = lax.broadcasted_iota(jnp.int32, (24, 128), 1)
    lane16 = lax.broadcasted_iota(jnp.int32, (16, 128), 1)

    @pl.loop(0, count)
    def _(s):
        assemble(where, big, s, phi)
        for x in range(XP):
            rows = [pl.ds(72 * x + 24 * b, 24) for b in range(3)]
            pr = [phi[0, r, :] for r in rows]
            pi = [phi[1, r, :] for r in rows]
            columns = []
            for n in range(OB):
                sr = [sec[0, n, r, :] for r in rows]
                si = [sec[1, n, r, :] for r in rows]
                for part in (
                    [pr[b] * sr[b] + pi[b] * si[b] for b in range(3)],
                    [pr[b] * si[b] - pi[b] * sr[b] for b in range(3)],
                ):
                    a, b, c = part
                    columns.append(
                        jnp.concatenate(
                            [
                                a,
                                pltpu.roll(jnp.where(lane < 96, b, a), 32, 1),
                                pltpu.roll(jnp.where(lane < 64, c, b), 64, 1),
                                pltpu.roll(c, 96, 1),
                            ],
                            axis=0,
                        )
                    )
            hi, lo = split(left(mat[...], jnp.concatenate(columns, axis=1)))
            for f in range(4):
                yw[f, pl.ds(G * x, G), 0:128] = hi[:, 128 * f : 128 * f + 128]
                yw[f, pl.ds(G * x, G), 128:256] = lo[:, 128 * f : 128 * f + 128]
        for f in range(4):
            p = dot(yw[f], wf[f])
            p = p[:, 0:128] + p[:, 128:256]
            if f:
                edge = 128 - 32 * f
                for x in range(XP):
                    for k in range(6):
                        r = G * x + 16 * k
                        start = 36 * count * (f - 1) + 36 * s + 6 * x + k
                        out[pl.ds(start, 16, stride=rt), :] = jnp.where(
                            lane16 < edge, held[pl.ds(r, 16), :], p[r : r + 16]
                        )
            if f < 3:
                held[...] = p


def middle_kernel(count, rec, table, mat1, mat2, out):
    rt = rows_per_dest(count)

    @pl.loop(0, count)
    def _(s):
        for kk in range(3):
            starts = [
                [36 * count * t + 36 * s + 6 * x + k for x in range(XP)]
                for k in (2 * kk, 2 * kk + 1)
                for t in range(3)
            ]
            v = jnp.concatenate(
                [
                    jnp.concatenate([rec[pl.ds(r, 16, stride=rt), :] for r in st], axis=0)
                    for st in starts
                ],
                axis=1,
            )
            v = left(mat2[...], v) * jnp.concatenate([table[2 * kk], table[2 * kk + 1]], axis=1)
            v = left(mat1[...], v)
            for i, st in enumerate(starts):
                for x in range(XP):
                    out[pl.ds(st[x], 16, stride=rt), :] = v[
                        16 * x : 16 * x + 16, 128 * i : 128 * i + 128
                    ]


def inverse_kernel(
    count, where, rec, big, image, sec, potim, mat, wi, delta, sums, phi, xw, wide, acc
):
    rt = rows_per_dest(count)
    lane = lax.broadcasted_iota(jnp.int32, (24, 128), 1)
    laneg = lax.broadcasted_iota(jnp.int32, (G, 128), 1)
    acc[...] = jnp.zeros_like(acc)

    @pl.loop(0, count)
    def _(s):
        assemble(where, big, s, phi)
        for x in range(XP):
            a, b, c = [
                jnp.concatenate(
                    [
                        rec[pl.ds(36 * count * t + 36 * s + 6 * x + k, 16, stride=rt), :]
                        for k in range(6)
                    ],
                    axis=0,
                )
                for t in range(3)
            ]
            fields = [a, jnp.where(laneg < 64, b, a), jnp.where(laneg < 32, c, b), c]
            for f in range(4):
                hi, lo = split(fields[f])
                xw[f, pl.ds(G * x, G), 0:128] = hi
                xw[f, pl.ds(G * x, G), 128:256] = lo
        for f in range(4):
            p = dot(xw[f], wi[f])
            wide[f] = p[:, 0:128] + p[:, 128:256]
        for x in range(XP):
            v = jnp.concatenate([wide[f, pl.ds(G * x, G), :] for f in range(4)], axis=1)
            v = left(mat[...], v)
            rows = [pl.ds(72 * x + 24 * b, 24) for b in range(3)]
            for n in range(OB):
                field = []
                for ri in range(2):
                    f = 2 * n + ri
                    y = [v[24 * i : 24 * i + 24, 128 * f : 128 * f + 128] for i in range(4)]
                    r1 = pltpu.roll(y[1], 96, 1)
                    r2 = pltpu.roll(y[2], 64, 1)
                    r3 = pltpu.roll(y[3], 32, 1)
                    field.append(
                        [
                            jnp.where(lane < 96, y[0], r1),
                            jnp.where(lane < 64, r1, r2),
                            jnp.where(lane < 32, r2, r3),
                        ]
                    )
                for b in range(3):
                    pr, pi = phi[0, rows[b], :], phi[1, rows[b], :]
                    vr, vi = field[0][b], field[1][b]
                    acc[0, n, rows[b], :] += pr * vr - pi * vi
                    acc[1, n, rows[b], :] += pr * vi + pi * vr

    def tail(i, carry):
        carry = list(carry)
        rows = pl.ds(pl.multiple_of(24 * i, 8), 24)
        v = potim[rows, :]
        for n in range(OB):
            re, im = image[0, n, rows, :], image[1, n, rows, :]
            sr, si = sec[0, n, rows, :], sec[1, n, rows, :]
            hr = v * sr + acc[0, n, rows, :]
            hi = v * si + acc[1, n, rows, :]
            dr = (0.5 * TIME_STEP) * (v * im + hi)
            di = (0.5 * TIME_STEP) * (-v * re - hr)
            delta[0, n, rows, :] = dr
            delta[1, n, rows, :] = di
            carry[n] = carry[n] + (re * dr + im * di)
            carry[2 + n] = carry[2 + n] + (dr * dr + di * di)
            carry[4 + n] = carry[4 + n] + (sr * hr + si * hi)
        return tuple(carry)

    zero = jnp.zeros((24, 128), F32)
    carry = lax.fori_loop(0, 18, tail, (zero,) * 6)
    rows = [jnp.sum(c, axis=0, keepdims=True) for c in carry]
    block = jnp.concatenate(rows + [jnp.zeros((2, 128), F32)], axis=0)
    for g in range(GRID):
        sums[g] = block


def stored_kernel(delta, out):
    @pl.loop(0, XP)
    def _(x):
        for c in range(2):
            for n in range(OB):
                for b in range(3):
                    rows = pl.ds(pl.multiple_of(72 * x + 24 * b, 8), 24)
                    out[pl.ds((c * XP + x) * 144 + 2 * b + n, 24, stride=6), :] = delta[
                        c, n, rows, :
                    ]


def final_kernel(filling, gathered, psi, delta, out, energies):
    t = jnp.sum(jnp.sum(gathered[...], axis=0), axis=1, keepdims=True)
    factor = -2.0 * t[0:2] / (t[2:4] + 1e-06)
    odd = lax.broadcasted_iota(jnp.int32, (216, 128), 0) % OB == 1
    scale = jnp.where(odd, factor[1:2], factor[0:1])

    @pl.loop(0, 8)
    def _(i):
        rows = pl.ds(pl.multiple_of(216 * i, 8), 216)
        out[rows, :] = psi[rows, :] + scale * delta[rows, :]

    for n in range(OB):
        energies[n] = filling[n] * t[4 + n, 0] / (G * G * G)


VM = pl.BlockSpec(memory_space=pltpu.VMEM)
SM = pl.BlockSpec(memory_space=pltpu.SMEM)


def shape(*dims):
    return jax.ShapeDtypeStruct(dims, F32)


def call(kernel, outs, ins, scratch=(), smem=0, flops=0, moved=0):
    return pl.pallas_call(
        kernel,
        out_shape=outs,
        in_specs=[SM] * smem + [VM] * (len(ins) - smem),
        out_specs=[VM] * len(outs),
        scratch_shapes=list(scratch),
        cost_estimate=pl.CostEstimate(flops=flops, bytes_accessed=moved, transcendentals=0),
    )(*ins)


def run_prepare(hi, lo):
    wide = jax.ShapeDtypeStruct((4, 256, 256), BF)
    return call(prepare_kernel, [wide, wide], [hi, lo], moved=2 << 20)


def run_section(psi, pot):
    return call(
        section_kernel,
        [shape(2, OB, 432, 128), shape(2, OB, 432, 128), shape(432, 128), shape(16, 112, 128)],
        [psi, pot],
        moved=4 << 20,
    )


def run_stored(delta):
    return call(stored_kernel, [shape(1728, 128)], [delta], moved=2 << 20)[0]


def run_final(filling, gathered, psi, delta):
    return pl.pallas_call(
        final_kernel,
        out_shape=[shape(1728, 128), shape(OB)],
        in_specs=[SM, VM, VM, VM],
        out_specs=[VM, SM],
        cost_estimate=pl.CostEstimate(flops=1 << 20, bytes_accessed=3 << 20, transcendentals=0),
    )(filling, gathered, psi, delta)


def run_forward(count, where, big, sec, mat, wf):
    rows = GRID * rows_per_dest(count)
    return call(
        functools.partial(forward_kernel, count),
        [shape(rows, 128)],
        [where, big, sec, mat, wf],
        [
            pltpu.VMEM((2, 432, 128), F32),
            pltpu.VMEM((4, XP * G, 256), BF),
            pltpu.VMEM((XP * G, 128), F32),
        ],
        smem=1,
        flops=count << 30,
        moved=count << 21,
    )[0]


def run_middle(count, rec, table, mat1, mat2):
    rows = GRID * rows_per_dest(count)
    return call(
        functools.partial(middle_kernel, count),
        [shape(rows, 128)],
        [rec, table, mat1, mat2],
        flops=count << 30,
        moved=count << 21,
    )[0]


def run_inverse(count, where, rec, big, image, sec, potim, mat, wi):
    return call(
        functools.partial(inverse_kernel, count),
        [shape(2, OB, 432, 128), shape(GRID, 8, 128)],
        [where, rec, big, image, sec, potim, mat, wi],
        [
            pltpu.VMEM((2, 432, 128), F32),
            pltpu.VMEM((4, XP * G, 256), BF),
            pltpu.VMEM((4, XP * G, 128), F32),
            pltpu.VMEM((2, OB, 432, 128), F32),
        ],
        smem=1,
        flops=count << 30,
        moved=count << 21,
    )


def screened_table(position):
    def fold(index):
        return jnp.where(index <= G // 2, index, index - G).astype(F32)

    step = 2.0 * math.pi / BOX
    fy = fold(6 * position + jnp.arange(6, dtype=jnp.int32))[:, None, None]
    fx = fold(jnp.arange(G, dtype=jnp.int32))[None, :, None]
    fz = fold(jnp.arange(4 * G, dtype=jnp.int32) % G)[None, None, :]
    wave = (step * step) * (fx * fx + fy * fy + fz * fz)
    safe = jnp.where(wave > 0, wave, 1.0)
    screen = -jnp.expm1(-wave / (4.0 * OMEGA * OMEGA)) / safe
    screen = jnp.where(wave > 0, screen, 1.0 / (4.0 * OMEGA * OMEGA))
    return screen * (-2.0 * MIXING / (G * G * G))


RIGHT = [(h * 8 + z, h * 8 + (z + 1) % 8) for h in range(2) for z in range(8)]
LEFT = [(d, s) for s, d in RIGHT]
SWAP = [(i, i ^ 8) for i in range(16)]


def gather_sources(pieces):
    hop = lambda v, pairs: lax.ppermute(v, "band", pairs)
    put = lambda big, v, i, part: lax.dynamic_update_slice(big, v[None, None], (i, part, 0, 0, 0))
    own_r, own_l, other = hop(pieces, RIGHT), hop(pieces, LEFT), hop(pieces, SWAP)
    big = put(jnp.zeros((8, 2) + pieces.shape, F32), pieces, 0, 0)

    def step(i, carry):
        own_r, own_l, other_r, other_l, big = carry
        big = put(big, own_l, i + 1, 0)
        big = put(big, own_r, 7 - i, 0)
        big = put(big, other_l, i, 1)
        big = put(big, other_r, (8 - i) & 7, 1)
        return (
            hop(own_r, RIGHT),
            hop(own_l, LEFT),
            hop(other_r, RIGHT),
            hop(other_l, LEFT),
            big,
        )

    carry = lax.fori_loop(0, 3, step, (own_r, own_l, other, other, big))
    _, own_l, other_r, other_l, big = carry
    far = hop(other_l, LEFT)
    big = put(big, own_l, 4, 0)
    big = put(big, other_l, 3, 1)
    big = put(big, other_r, 5, 1)
    return put(big, far, 4, 1)


def per_device(orbitals, local_potential, plan, occupancy):
    group = jnp.arange(GROUPS, dtype=jnp.int32)
    lookup = lambda g: jnp.sum(jnp.where(group == g, occupancy, 0))
    band = lax.axis_index("band")
    where = jnp.stack([band % 8, band // 8]).astype(jnp.int32)
    (mat_fy, mat_fx, mat_ix, mat_iy), (hi, lo) = jax.tree.map(jnp.asarray, tables())
    wf, wi = run_prepare(hi, lo)
    tiled = orbitals.reshape(2, OB, XP, 72, 128).transpose(0, 2, 3, 1, 4).reshape(-1, 128)
    table = screened_table(lax.axis_index("grid"))
    sec, image, potim, pay = run_section(tiled, local_potential)
    pool = lax.all_to_all(pay, "band", 0, 0, tiled=True)
    first, second = lookup(plan[0]), lookup(plan[1])
    third = jnp.where(first > 1, plan[0], plan[1])
    slots = [(plan[0], 0), (plan[1], 0), (third, 1), (plan[1], 1)]
    chosen = jnp.stack(
        [lax.dynamic_slice(pool, (g, 56 * j, 0), (1, 56, 128))[0] for g, j in slots]
    )

    def branch(count):
        def run(sec, image, potim, chosen, table, wf, wi):
            pieces = chosen[:count]
            big = gather_sources(pieces)
            send = run_forward(count, where, big, sec, mat_fy, wf)
            got = lax.all_to_all(send, "grid", 0, 0, tiled=True)
            back = run_middle(count, got, table, mat_ix, mat_fx)
            got = lax.all_to_all(back, "grid", 0, 0, tiled=True)
            return tuple(run_inverse(count, where, got, big, image, sec, potim, mat_iy, wi))

        return run

    delta, sums = lax.switch(
        first + second - 2,
        [branch(2), branch(3), branch(4)],
        sec,
        image,
        potim,
        chosen,
        table,
        wf,
        wi,
    )
    gathered = lax.all_to_all(sums, "grid", 0, 0, tiled=True)
    own_filled = lookup(band)
    filling = jnp.where(jnp.arange(OB, dtype=jnp.int32) < own_filled, 2.0, 0.0).astype(F32)
    fresh, energies = run_final(filling, gathered, tiled, run_stored(delta))
    fresh = fresh.reshape(2, XP, 72, OB, 128)
    fresh = fresh.transpose(0, 3, 1, 2, 4).reshape(orbitals.shape)
    return (fresh, energies)


def solution(mesh):
    return jax.shard_map(
        per_device,
        mesh=mesh,
        in_specs=(P(None, "band", "grid", None), P("grid", None), P(), P()),
        out_specs=(P(None, "band", "grid", None), P("band")),
        check_vma=False,
    )
```

```python
import functools
import math

import jax
import jax.numpy as jnp
import numpy as np
from jax import lax
from jax.experimental import pallas as pl
from jax.experimental.pallas import tpu as pltpu
from jax.sharding import PartitionSpec as P

G = 96
XP = 6
OB = 2
GROUPS = 16
GRID = 16
LANES = G * G
TIME_STEP = 0.4
MIXING = 0.25
OMEGA = 0.106
BOX = 65.1
BF = jnp.bfloat16
F32 = jnp.float32


def tables():
    index = np.arange(G)
    angle = (index[:, None] * index[None, :] % G) * (2.0 * math.pi / G)
    cas = np.cos(angle) + np.sin(angle)
    perm = np.array([6 * (i % 16) + i // 16 for i in range(G)])

    def halves(m):
        hi = np.asarray(m, np.float32).astype(jnp.bfloat16)
        lo = (m - hi.astype(np.float64)).astype(np.float32).astype(jnp.bfloat16)
        return hi, lo

    def extend(m):
        hi, lo = halves(m)
        return np.block([[hi, hi], [lo, np.zeros_like(lo)]])

    rows = np.array([4 * (i % 24) + i // 24 for i in range(G)])
    pads = [np.pad(h.astype(np.float32), (0, 128 - G)) for h in halves(cas)]
    mats = [cas[perm][:, rows], cas[:, perm], cas[perm], cas[rows][:, perm]]
    return [extend(m) for m in mats], pads


def split(v):
    hi = v.astype(BF)
    return hi, (v - hi.astype(F32)).astype(BF)


def dot(a, b):
    return jnp.dot(a, b, preferred_element_type=F32)


def left(mat, v):
    hi, lo = split(v)
    p = dot(mat, jnp.concatenate([hi, lo], axis=0))
    return p[:G] + p[G:]


def rows_per_dest(count):
    return -(-3 * 36 * count // 8) * 8


def prepare_kernel(hi, lo, wf, wi):
    zero = jnp.zeros((128, 128), BF)
    for f in range(4):
        for axis, out in ((1, wf), (0, wi)):
            shift = 96 * f % 128
            h = (pltpu.roll(hi[...], shift, axis) if shift else hi[...]).astype(BF)
            l = (pltpu.roll(lo[...], shift, axis) if shift else lo[...]).astype(BF)
            out[f, 0:128, 0:128] = h
            out[f, 128:256, 0:128] = h
            out[f, 0:128, 128:256] = l
            out[f, 128:256, 128:256] = zero


def section_kernel(psi, pot, sec, image, potim, pay):
    for t in range(72):
        a, b = t // 3, t % 3
        potim[pl.ds(24 * b + a, XP, stride=72), :] = pot[:, 128 * t : 128 * t + 128]

    @pl.loop(0, XP)
    def _(x):
        for b in range(3):
            rows = pl.ds(pl.multiple_of(72 * x + 24 * b, 8), 24)
            v = TIME_STEP * potim[rows, :]
            for n in range(OB):
                re, im = [
                    psi[pl.ds((c * XP + x) * 144 + 2 * b + n, 24, stride=6), :] for c in range(2)
                ]
                sec[0, n, rows, :] = re + v * im
                sec[1, n, rows, :] = im - v * re
                image[0, n, rows, :] = re
                image[1, n, rows, :] = im

    for c in range(2):
        for n in range(OB):
            for q in range(8):
                pay[8 * c + q, 56 * n : 56 * n + 54, :] = sec[c, n, 54 * q : 54 * q + 54, :]


def assemble(where, big, s, phi):
    for c in range(2):
        for q in range(8):
            rel = (q + 8 - where[0]) & 7
            phi[c, 54 * q : 54 * q + 54, :] = big[rel, c ^ where[1], s, 0:54, :]


def forward_kernel(count, where, big, sec, mat, wf, out, phi, yw, held):
    rt = rows_per_dest(count)
    lane = lax.broadcasted_iota(jnp.int32, (24, 128), 1)
    lane16 = lax.broadcasted_iota(jnp.int32, (16, 128), 1)

    @pl.loop(0, count)
    def _(s):
        assemble(where, big, s, phi)
        for x in range(XP):
            rows = [pl.ds(72 * x + 24 * b, 24) for b in range(3)]
            pr = [phi[0, r, :] for r in rows]
            pi = [phi[1, r, :] for r in rows]
            columns = []
            for n in range(OB):
                sr = [sec[0, n, r, :] for r in rows]
                si = [sec[1, n, r, :] for r in rows]
                for part in (
                    [pr[b] * sr[b] + pi[b] * si[b] for b in range(3)],
                    [pr[b] * si[b] - pi[b] * sr[b] for b in range(3)],
                ):
                    a, b, c = part
                    columns.append(
                        jnp.concatenate(
                            [
                                a,
                                pltpu.roll(jnp.where(lane < 96, b, a), 32, 1),
                                pltpu.roll(jnp.where(lane < 64, c, b), 64, 1),
                                pltpu.roll(c, 96, 1),
                            ],
                            axis=0,
                        )
                    )
            hi, lo = split(left(mat[...], jnp.concatenate(columns, axis=1)))
            for f in range(4):
                yw[f, pl.ds(G * x, G), 0:128] = hi[:, 128 * f : 128 * f + 128]
                yw[f, pl.ds(G * x, G), 128:256] = lo[:, 128 * f : 128 * f + 128]
        for f in range(4):
            p = dot(yw[f], wf[f])
            p = p[:, 0:128] + p[:, 128:256]
            if f:
                edge = 128 - 32 * f
                for x in range(XP):
                    for k in range(6):
                        r = G * x + 16 * k
                        start = 36 * count * (f - 1) + 36 * s + 6 * x + k
                        out[pl.ds(start, 16, stride=rt), :] = jnp.where(
                            lane16 < edge, held[pl.ds(r, 16), :], p[r : r + 16]
                        )
            if f < 3:
                held[...] = p


def middle_kernel(count, rec, table, mat1, mat2, out):
    rt = rows_per_dest(count)

    @pl.loop(0, count)
    def _(s):
        for kk in range(3):
            starts = [
                [36 * count * t + 36 * s + 6 * x + k for x in range(XP)]
                for k in (2 * kk, 2 * kk + 1)
                for t in range(3)
            ]
            v = jnp.concatenate(
                [
                    jnp.concatenate([rec[pl.ds(r, 16, stride=rt), :] for r in st], axis=0)
                    for st in starts
                ],
                axis=1,
            )
            v = left(mat2[...], v) * jnp.concatenate([table[2 * kk], table[2 * kk + 1]], axis=1)
            v = left(mat1[...], v)
            for i, st in enumerate(starts):
                for x in range(XP):
                    out[pl.ds(st[x], 16, stride=rt), :] = v[
                        16 * x : 16 * x + 16, 128 * i : 128 * i + 128
                    ]


def inverse_kernel(
    count, where, rec, big, image, sec, potim, mat, wi, delta, sums, phi, xw, wide, acc
):
    rt = rows_per_dest(count)
    lane = lax.broadcasted_iota(jnp.int32, (24, 128), 1)
    laneg = lax.broadcasted_iota(jnp.int32, (G, 128), 1)
    acc[...] = jnp.zeros_like(acc)

    @pl.loop(0, count)
    def _(s):
        assemble(where, big, s, phi)
        for x in range(XP):
            a, b, c = [
                jnp.concatenate(
                    [
                        rec[pl.ds(36 * count * t + 36 * s + 6 * x + k, 16, stride=rt), :]
                        for k in range(6)
                    ],
                    axis=0,
                )
                for t in range(3)
            ]
            fields = [a, jnp.where(laneg < 64, b, a), jnp.where(laneg < 32, c, b), c]
            for f in range(4):
                hi, lo = split(fields[f])
                xw[f, pl.ds(G * x, G), 0:128] = hi
                xw[f, pl.ds(G * x, G), 128:256] = lo
        for f in range(4):
            p = dot(xw[f], wi[f])
            wide[f] = p[:, 0:128] + p[:, 128:256]
        for x in range(XP):
            v = jnp.concatenate([wide[f, pl.ds(G * x, G), :] for f in range(4)], axis=1)
            v = left(mat[...], v)
            rows = [pl.ds(72 * x + 24 * b, 24) for b in range(3)]
            for n in range(OB):
                field = []
                for ri in range(2):
                    f = 2 * n + ri
                    y = [v[24 * i : 24 * i + 24, 128 * f : 128 * f + 128] for i in range(4)]
                    r1 = pltpu.roll(y[1], 96, 1)
                    r2 = pltpu.roll(y[2], 64, 1)
                    r3 = pltpu.roll(y[3], 32, 1)
                    field.append(
                        [
                            jnp.where(lane < 96, y[0], r1),
                            jnp.where(lane < 64, r1, r2),
                            jnp.where(lane < 32, r2, r3),
                        ]
                    )
                for b in range(3):
                    pr, pi = phi[0, rows[b], :], phi[1, rows[b], :]
                    vr, vi = field[0][b], field[1][b]
                    acc[0, n, rows[b], :] += pr * vr - pi * vi
                    acc[1, n, rows[b], :] += pr * vi + pi * vr

    def tail(i, carry):
        carry = list(carry)
        rows = pl.ds(pl.multiple_of(24 * i, 8), 24)
        v = potim[rows, :]
        for n in range(OB):
            re, im = image[0, n, rows, :], image[1, n, rows, :]
            sr, si = sec[0, n, rows, :], sec[1, n, rows, :]
            hr = v * sr + acc[0, n, rows, :]
            hi = v * si + acc[1, n, rows, :]
            dr = (0.5 * TIME_STEP) * (v * im + hi)
            di = (0.5 * TIME_STEP) * (-v * re - hr)
            delta[0, n, rows, :] = dr
            delta[1, n, rows, :] = di
            carry[n] = carry[n] + (re * dr + im * di)
            carry[2 + n] = carry[2 + n] + (dr * dr + di * di)
            carry[4 + n] = carry[4 + n] + (sr * hr + si * hi)
        return tuple(carry)

    zero = jnp.zeros((24, 128), F32)
    carry = lax.fori_loop(0, 18, tail, (zero,) * 6)
    rows = [jnp.sum(c, axis=0, keepdims=True) for c in carry]
    block = jnp.concatenate(rows + [jnp.zeros((2, 128), F32)], axis=0)
    for g in range(GRID):
        sums[g] = block


def stored_kernel(delta, out):
    @pl.loop(0, XP)
    def _(x):
        for c in range(2):
            for n in range(OB):
                for b in range(3):
                    rows = pl.ds(pl.multiple_of(72 * x + 24 * b, 8), 24)
                    out[pl.ds((c * XP + x) * 144 + 2 * b + n, 24, stride=6), :] = delta[
                        c, n, rows, :
                    ]


def final_kernel(filling, gathered, psi, delta, out, energies):
    t = jnp.sum(jnp.sum(gathered[...], axis=0), axis=1, keepdims=True)
    factor = -2.0 * t[0:2] / (t[2:4] + 1e-06)
    odd = lax.broadcasted_iota(jnp.int32, (216, 128), 0) % OB == 1
    scale = jnp.where(odd, factor[1:2], factor[0:1])

    @pl.loop(0, 8)
    def _(i):
        rows = pl.ds(pl.multiple_of(216 * i, 8), 216)
        out[rows, :] = psi[rows, :] + scale * delta[rows, :]

    for n in range(OB):
        energies[n] = filling[n] * t[4 + n, 0] / (G * G * G)


VM = pl.BlockSpec(memory_space=pltpu.VMEM)
SM = pl.BlockSpec(memory_space=pltpu.SMEM)


def shape(*dims):
    return jax.ShapeDtypeStruct(dims, F32)


def call(kernel, outs, ins, scratch=(), smem=0, flops=0, moved=0):
    return pl.pallas_call(
        kernel,
        out_shape=outs,
        in_specs=[SM] * smem + [VM] * (len(ins) - smem),
        out_specs=[VM] * len(outs),
        scratch_shapes=list(scratch),
        cost_estimate=pl.CostEstimate(flops=flops, bytes_accessed=moved, transcendentals=0),
    )(*ins)


def run_prepare(hi, lo):
    wide = jax.ShapeDtypeStruct((4, 256, 256), BF)
    return call(prepare_kernel, [wide, wide], [hi, lo], moved=2 << 20)


def run_section(psi, pot):
    return call(
        section_kernel,
        [shape(2, OB, 432, 128), shape(2, OB, 432, 128), shape(432, 128), shape(16, 112, 128)],
        [psi, pot],
        moved=4 << 20,
    )


def run_stored(delta):
    return call(stored_kernel, [shape(1728, 128)], [delta], moved=2 << 20)[0]


def run_final(filling, gathered, psi, delta):
    return pl.pallas_call(
        final_kernel,
        out_shape=[shape(1728, 128), shape(OB)],
        in_specs=[SM, VM, VM, VM],
        out_specs=[VM, SM],
        cost_estimate=pl.CostEstimate(flops=1 << 20, bytes_accessed=3 << 20, transcendentals=0),
    )(filling, gathered, psi, delta)


def run_forward(count, where, big, sec, mat, wf):
    rows = GRID * rows_per_dest(count)
    return call(
        functools.partial(forward_kernel, count),
        [shape(rows, 128)],
        [where, big, sec, mat, wf],
        [
            pltpu.VMEM((2, 432, 128), F32),
            pltpu.VMEM((4, XP * G, 256), BF),
            pltpu.VMEM((XP * G, 128), F32),
        ],
        smem=1,
        flops=count << 30,
        moved=count << 21,
    )[0]


def run_middle(count, rec, table, mat1, mat2):
    rows = GRID * rows_per_dest(count)
    return call(
        functools.partial(middle_kernel, count),
        [shape(rows, 128)],
        [rec, table, mat1, mat2],
        flops=count << 30,
        moved=count << 21,
    )[0]


def run_inverse(count, where, rec, big, image, sec, potim, mat, wi):
    return call(
        functools.partial(inverse_kernel, count),
        [shape(2, OB, 432, 128), shape(GRID, 8, 128)],
        [where, rec, big, image, sec, potim, mat, wi],
        [
            pltpu.VMEM((2, 432, 128), F32),
            pltpu.VMEM((4, XP * G, 256), BF),
            pltpu.VMEM((4, XP * G, 128), F32),
            pltpu.VMEM((2, OB, 432, 128), F32),
        ],
        smem=1,
        flops=count << 30,
        moved=count << 21,
    )


def screened_table(position):
    def fold(index):
        return jnp.where(index <= G // 2, index, index - G).astype(F32)

    step = 2.0 * math.pi / BOX
    fy = fold(6 * position + jnp.arange(6, dtype=jnp.int32))[:, None, None]
    fx = fold(jnp.arange(G, dtype=jnp.int32))[None, :, None]
    fz = fold(jnp.arange(4 * G, dtype=jnp.int32) % G)[None, None, :]
    wave = (step * step) * (fx * fx + fy * fy + fz * fz)
    safe = jnp.where(wave > 0, wave, 1.0)
    screen = -jnp.expm1(-wave / (4.0 * OMEGA * OMEGA)) / safe
    screen = jnp.where(wave > 0, screen, 1.0 / (4.0 * OMEGA * OMEGA))
    return screen * (-2.0 * MIXING / (G * G * G))


RIGHT = [(h * 8 + z, h * 8 + (z + 1) % 8) for h in range(2) for z in range(8)]
LEFT = [(d, s) for s, d in RIGHT]
SWAP = [(i, i ^ 8) for i in range(16)]


def gather_sources(pieces):
    hop = lambda v, pairs: lax.ppermute(v, "band", pairs)
    both = jnp.stack([pieces, hop(pieces, SWAP)])

    def step(i, carry):
        right, left, big = carry
        big = lax.dynamic_update_index_in_dim(big, left, i, 0)
        big = lax.dynamic_update_index_in_dim(big, right, (8 - i) % 8, 0)
        return hop(right, RIGHT), hop(left, LEFT), big

    big = jnp.zeros((8,) + both.shape, F32)
    _, left, big = lax.fori_loop(0, 4, step, (both, both, big))
    return lax.dynamic_update_index_in_dim(big, left, 4, 0)


def gather_apart(pieces):
    hop = lambda v, pairs: lax.ppermute(v, "band", pairs)

    def ring(v, last):
        r1, l1 = hop(v, RIGHT), hop(v, LEFT)
        r2, l2 = hop(r1, RIGHT), hop(l1, LEFT)
        r3, l3 = hop(r2, RIGHT), hop(l2, LEFT)
        far = hop(r3, RIGHT) if last else hop(l3, LEFT)
        return [v, l1, l2, l3, far, r3, r2, r1]

    own = ring(pieces, True)
    other = ring(hop(pieces, SWAP), False)
    return jnp.stack([jnp.stack(pair) for pair in zip(own, other)])


def per_device(orbitals, local_potential, plan, occupancy):
    group = jnp.arange(GROUPS, dtype=jnp.int32)
    lookup = lambda g: jnp.sum(jnp.where(group == g, occupancy, 0))
    band = lax.axis_index("band")
    where = jnp.stack([band % 8, band // 8]).astype(jnp.int32)
    (mat_fy, mat_fx, mat_ix, mat_iy), (hi, lo) = jax.tree.map(jnp.asarray, tables())
    wf, wi = run_prepare(hi, lo)
    tiled = orbitals.reshape(2, OB, XP, 72, 128).transpose(0, 2, 3, 1, 4).reshape(-1, 128)
    table = screened_table(lax.axis_index("grid"))
    sec, image, potim, pay = run_section(tiled, local_potential)
    pool = lax.all_to_all(pay, "band", 0, 0, tiled=True)
    first, second = lookup(plan[0]), lookup(plan[1])
    third = jnp.where(first > 1, plan[0], plan[1])
    slots = [(plan[0], 0), (plan[1], 0), (third, 1), (plan[1], 1)]
    chosen = jnp.stack(
        [lax.dynamic_slice(pool, (g, 56 * j, 0), (1, 56, 128))[0] for g, j in slots]
    )

    def branch(count):
        def run(sec, image, potim, chosen, table, wf, wi):
            pieces = chosen[:count]
            big = gather_apart(pieces) if count == 3 else gather_sources(pieces)
            send = run_forward(count, where, big, sec, mat_fy, wf)
            got = lax.all_to_all(send, "grid", 0, 0, tiled=True)
            back = run_middle(count, got, table, mat_ix, mat_fx)
            got = lax.all_to_all(back, "grid", 0, 0, tiled=True)
            return tuple(run_inverse(count, where, got, big, image, sec, potim, mat_iy, wi))

        return run

    delta, sums = lax.switch(
        first + second - 2,
        [branch(2), branch(3), branch(4)],
        sec,
        image,
        potim,
        chosen,
        table,
        wf,
        wi,
    )
    gathered = lax.all_to_all(sums, "grid", 0, 0, tiled=True)
    own_filled = lookup(band)
    filling = jnp.where(jnp.arange(OB, dtype=jnp.int32) < own_filled, 2.0, 0.0).astype(F32)
    fresh, energies = run_final(filling, gathered, tiled, run_stored(delta))
    fresh = fresh.reshape(2, XP, 72, OB, 128)
    fresh = fresh.transpose(0, 3, 1, 2, 4).reshape(orbitals.shape)
    return (fresh, energies)


def solution(mesh):
    return jax.shard_map(
        per_device,
        mesh=mesh,
        in_specs=(P(None, "band", "grid", None), P("grid", None), P(), P()),
        out_specs=(P(None, "band", "grid", None), P("band")),
        check_vma=False,
    )
```
